128 devices in a mesh: seq: 2 (over core), expert: 8 (over z_hi, x), tensor: 8 (over y, z_lo).
Axes of the slice: x: 4, y: 4, z: 4 (z_hi: 2, z_lo: 2; z = z_hi * 2 + z_lo), core: 2. Of those that a mesh axis runs over, the one named last changes fastest.
Arguments:
- tokens: bfloat16 [2048, 4096], P(('seq', 'expert'), 'tensor'), may hold values from -100 to 100
- routes: int32 [2048, 2], P(('seq', 'expert')), may hold values from 0 to 7, all different within a row; in each aligned block of 128 rows (0 to 127, 128 to 255, ...) at most 64 rows name the same one
- route_weights: float32 [2048, 2], P(('seq', 'expert')), may hold values from 0.1 to 0.9
- norm_gain: float32 [4096], P('tensor'), may hold values from 0.1 to 1.9
- final_gain: float32 [4096], P('tensor'), may hold values from 0.1 to 1.9
- w_gate: bfloat16 [8, 4096, 14336], P('expert', None, ('seq', 'tensor')), may hold values from -0.09375 to 0.09375
- w_up: bfloat16 [8, 4096, 14336], P('expert', None, ('seq', 'tensor')), may hold values from -0.09375 to 0.09375
- w_down: bfloat16 [8, 14336, 4096], P('expert', ('seq', 'tensor')), may hold values from -0.09375 to 0.09375
- head_weight: bfloat16 [4096, 32000], P(None, ('expert', 'tensor')), may hold values from -100 to 100
- targets: int32 [2048], P('seq'), may hold values from 0 to 31999
Outputs:
- loss: float32 [2048], P(('seq', 'expert', 'tensor'))
The draws below stay inside these ranges and needn't reach their ends.
Inputs may be any that keep to these rules, and one draw needn't show every extreme that they name: Within each aligned block of 128 rows no expert is named by more than 64 routes, a bound that some block reaches; the two experts of a row differ.
All inputs are finite; a program needn't handle non-finite values.
Results may differ from the reference program's by a relative error of at most 0.00365.
Values may be sent and summed in bfloat16 or wider, within the bound.
A program may use at most 192 MiB of HBM per device.

```python
import math
import jax
import jax.numpy as jnp
import numpy as np
from jax import lax

D = 4096
FF = 14336
VOCAB = 32000
TOPK = 2
TOK_DEV = 128
EXPERTS = 8
CAP = 64
TOKENS = 2048


def draw_tokens(key, part):
    key_base, key_column, key_row = jax.random.split(key, 3)
    column = jnp.arange(D, dtype=jnp.float32) / D
    column_scale = (3.0 ** column)[None, :] * jnp.exp(jax.random.uniform(key_column, (1, D), minval=0.0, maxval=1.1))
    base_draw = jax.random.truncated_normal(key_base, -4.0, 4.0, (TOKENS, D))
    row_scale = jnp.exp(jax.random.uniform(key_row, (TOKENS, 1), minval=0.0, maxval=math.log(10.0)))
    values = 0.15 * row_scale * base_draw * column_scale
    return values.astype(jnp.bfloat16)


def draw_head_weight(key, part):
    key_base = jax.random.fold_in(key, 0)
    base_draw = jax.random.truncated_normal(key_base, -4.0, 4.0, (D, VOCAB)) * (3.0 * D ** (-0.5))
    values = base_draw
    return values.astype(jnp.bfloat16)


def plant(values, key, low, high):
    longest = values.shape.index(max(values.shape))
    spots = []
    for shift in (0, 1):
        where = [jax.random.randint(jax.random.fold_in(key, axis), (), 0, length) for axis, length in enumerate(values.shape)]
        where[longest] = (where[longest] + shift) % values.shape[longest]
        spots.append(tuple(where))
    return values.at[spots[0]].set(low).at[spots[1]].set(high)


def block_scale(key, extent, pieces, least, largest):
    def one(position, shards_of):
        steps = jax.random.uniform(jax.random.fold_in(jax.random.fold_in(key, 6), position), (shards_of,), jnp.float32, least / len(pieces), largest / len(pieces))
        return jnp.repeat(jnp.exp(steps), extent[position] // shards_of).reshape((-1,) + (1,) * (len(extent) - position - 1))

    factor_of = one(*pieces[0])
    for cut in pieces[1:]:
        factor_of = factor_of * one(*cut)
    return factor_of


def rank_bounds(number_of, slope):
    loads = [(1 << 20) // math.isqrt(rank ** slope) + 1 for rank in range(1, number_of + 1)]
    width = 1 + sum(loads) // (1 << 30)
    return np.cumsum(np.array([max(1, weight // width) for weight in loads]))


def ranked_ids(key, shape, count, lean):
    listing = rank_bounds(count, lean)
    ticket = jax.random.randint(jax.random.fold_in(key, 1), shape, 0, int(listing[count - 1]))
    rank = jnp.searchsorted(jnp.asarray(listing, jnp.int32), ticket, side="right")
    return jax.random.permutation(jax.random.fold_in(key, 2), count)[rank].astype(jnp.int32)


def assign_block(key, own, number, rows, number_of, top, most, slope):
    sequence = jax.random.permutation(key, number_of)
    packed, common = portions_of(number_of, rows * top, most, slope, True), portions_of(number_of, rows * top, most, slope, False)
    places = jnp.arange(number_of)

    def named(tallies, offset_by):
        used = int((tallies > 0).sum())
        fixed = max(1, used // 4)
        moved = fixed + (places - fixed + offset_by * (used - fixed)) % max(1, number_of - fixed)
        return jnp.zeros((number_of,), jnp.int32).at[sequence[jnp.where(places < fixed, places, moved)]].set(jnp.asarray(tallies, jnp.int32))

    tallies = jnp.where(number % 4 == 0, named(packed, number // 4), named(common, number - number // 4 - 1))
    mixed = jax.random.permutation(jax.random.fold_in(own, 3), number_of)
    source_of, taker = mixed[0:number_of // 2 * 2:2], mixed[1:number_of // 2 * 2:2]
    room = jnp.minimum(tallies[source_of] - 1, most - tallies[taker]) // 2
    room = jnp.where((source_of == sequence[0]) | (taker == sequence[0]) | (tallies[taker] == 0), 0, jnp.maximum(room, 0))
    moved = jax.random.randint(jax.random.fold_in(own, 4), (number_of // 2,), 0, 1 << 20) % (room + 1)
    tallies = tallies.at[source_of].add(-moved).at[taker].add(moved)
    labels = jnp.searchsorted(jnp.cumsum(tallies), jnp.arange(rows * top), side="right").astype(jnp.int32)
    table = labels.reshape(top, rows).T
    table = table[jax.random.permutation(jax.random.fold_in(own, 1), rows)]
    offset_by = jax.random.randint(jax.random.fold_in(own, 2), (rows, 1), 0, top)
    return jnp.take_along_axis(table, (jnp.arange(top)[None, :] + offset_by) % top, axis=1)


def portions_of(count, total, most, lean, full):
    portions = [(1 << 20) // math.isqrt(grade ** lean) + 1 for grade in range(1, count + 1)]
    largest = most if full else min(most, max(-(-total // count), total * portions[0] // sum(portions)))
    least = 1 if total - largest >= count - 1 else 0
    counts, rest = [largest] + [least] * (count - 1), total - largest - least * (count - 1)
    while rest > 0:
        free = [i for i in range(1, count) if counts[i] < largest] or [i for i in range(1, count) if counts[i] < most]
        whole, remaining = sum([portions[i] for i in free]), rest
        for i in free:
            addition = min(most - counts[i], max(1, remaining * portions[i] // whole), rest)
            counts[i] = counts[i] + addition
            rest = rest - addition
    return np.array(counts)


def scatter_about(rng, shape, deviation, reach, cuts=(), kind=jnp.bfloat16):
    drawn = jax.random.normal(rng, shape, jnp.float32) * deviation
    if len(cuts) > 0:
        drawn = block_scale(rng, shape, cuts, -0.22, 0.18) * drawn
    return jnp.clip(drawn, min=-reach, max=reach).astype(kind)


def setup_inputs(seed: int = 0) -> dict:
    seeds = jax.random.split(jax.random.key(seed), 11)
    tokens = draw_tokens(jax.random.fold_in(seeds[10], 71), 0)
    routes_keys = jax.random.split(jax.random.fold_in(seeds[1], 1), TOKENS // TOK_DEV)
    routes_turns = jax.random.permutation(jax.random.fold_in(seeds[1], 3), TOKENS // TOK_DEV)
    routes = jax.vmap(lambda own, number: assign_block(jax.random.fold_in(seeds[1], 2), own, number, TOK_DEV, EXPERTS, TOPK, CAP, 2))(routes_keys, routes_turns).reshape((TOKENS, TOPK))
    route_weights = jnp.clip(0.1 + 0.79999997 * jax.random.uniform(seeds[2], (TOKENS, TOPK), jnp.float32) ** block_scale(seeds[2], (TOKENS, TOPK), ((0, 16),), -0.2, 0.2), 0.1, 0.9)
    norm_gain = jnp.clip(1.0 + 0.18 * jax.random.normal(seeds[3], (D,), jnp.float32), 0.1, 1.9)
    final_gain = jnp.clip(1.0 + 0.18 * jax.random.normal(seeds[4], (D,), jnp.float32), 0.1, 1.9)
    w_gate = scatter_about(seeds[5], (EXPERTS, D, FF), D ** -0.5, 0.09375, ((0, 8), (2, 16)))
    w_up = scatter_about(seeds[6], (EXPERTS, D, FF), D ** -0.5, 0.09375, ((0, 8), (2, 16)))
    w_down = scatter_about(seeds[7], (EXPERTS, FF, D), (FF // 4) ** -0.5, 0.09375, ((0, 8), (1, 16)))
    head_weight = draw_head_weight(jax.random.fold_in(seeds[10], 71), 0)
    targets = plant(ranked_ids(seeds[9], (TOKENS,), VOCAB, 2), jax.random.fold_in(seeds[9], 3), 0, VOCAB - 1).astype(jnp.int32)
    return {"tokens": tokens, "routes": routes, "route_weights": route_weights, "norm_gain": norm_gain, "final_gain": final_gain, "w_gate": w_gate, "w_up": w_up, "w_down": w_down, "head_weight": head_weight, "targets": targets}


epsilon = 1e-05

def reference(tokens, routes, route_weights, norm_gain, final_gain, w_gate, w_up, w_down, head_weight, targets):
    token_float = tokens.astype(jnp.float32)
    normed = (token_float * lax.rsqrt(lax.optimization_barrier(jnp.mean(token_float * token_float, axis=1, keepdims=True)) + epsilon) * norm_gain[None, :]).astype(jnp.bfloat16)
    flat_routes = routes.reshape(-1)
    flat_weights = route_weights.reshape(-1)
    limit = TOKENS // TOK_DEV * CAP

    def per_expert(mixed_rows, expert_id):
        keys = (flat_routes != expert_id).astype(jnp.int32)
        row_order = jnp.argsort(keys, stable=True)[:limit].astype(jnp.int32)
        token_index = row_order // 2
        row_block = normed[token_index].astype(jnp.float32)
        gate_mat = lax.dynamic_index_in_dim(w_gate, expert_id, 0, False).astype(jnp.float32)
        up_mat = lax.dynamic_index_in_dim(w_up, expert_id, 0, False).astype(jnp.float32)
        down_mat = lax.dynamic_index_in_dim(w_down, expert_id, 0, False).astype(jnp.float32)
        gate_part = jnp.dot(row_block, gate_mat, precision=lax.Precision.HIGHEST)
        up_part = jnp.dot(row_block, up_mat, precision=lax.Precision.HIGHEST)
        hidden = (jax.nn.silu(gate_part) * up_part).astype(jnp.bfloat16)
        expert_out = jnp.dot(hidden.astype(jnp.float32), down_mat, precision=lax.Precision.HIGHEST).astype(jnp.bfloat16)
        is_live = flat_routes[row_order] == expert_id
        weight_live = jnp.where(is_live, flat_weights[row_order], jnp.zeros_like(flat_weights[row_order]))
        mixed_rows = mixed_rows.at[token_index].add(weight_live[:, None] * expert_out.astype(jnp.float32))
        return (mixed_rows, None)
    mixed_start = jnp.zeros(token_float.shape, jnp.float32)
    mixed_rows, unused = lax.scan(per_expert, mixed_start, jnp.arange(EXPERTS, dtype=jnp.int32))
    residual = (token_float + mixed_rows).astype(jnp.bfloat16)
    residual_float = residual.astype(jnp.float32)
    final_rows = (residual_float * lax.rsqrt(lax.optimization_barrier(jnp.mean(residual_float * residual_float, axis=1, keepdims=True)) + epsilon) * final_gain[None, :]).astype(jnp.bfloat16)
    logits = jnp.dot(final_rows.astype(jnp.float32), head_weight.astype(jnp.float32), precision=lax.Precision.HIGHEST)
    row_top = lax.optimization_barrier(jnp.max(logits, axis=1))
    row_total = lax.optimization_barrier(jnp.sum(jnp.exp(logits - row_top[:, None]), axis=1))
    target_logit = jnp.take_along_axis(logits, targets[:, None].astype(jnp.int32), axis=1)[:, 0]
    return row_top + jnp.log(row_total) - target_logit
```

```python
import jax
import jax.numpy as jnp
from jax import lax
from jax.sharding import PartitionSpec as P

epsilon = 1e-05


def merge_terms(stacked):
    top = jnp.max(stacked[:, 0], axis=0)
    total = jnp.sum(stacked[:, 1] * jnp.exp(stacked[:, 0] - top[None]), axis=0)
    return jnp.stack([top, total, jnp.sum(stacked[:, 2], axis=0)])


def on_device(
    tokens, routes, route_weights, norm_gain, final_gain, w_gate, w_up, w_down, head_weight, targets
):
    tok_rows, slice_width = tokens.shape
    n_seq = lax.axis_size("seq")
    n_expert = lax.axis_size("expert")
    n_tensor = lax.axis_size("tensor")
    full_width = slice_width * n_tensor
    experts = w_gate.shape[0] * n_expert
    capacity = 4 * tok_rows // experts
    slots_all = experts * capacity
    vocab_part = head_weight.shape[1]
    token_float = tokens.astype(jnp.float32)
    first_squares = lax.psum(jnp.sum(token_float * token_float, axis=1), "tensor")
    normed = (
        token_float * lax.rsqrt(first_squares / full_width + epsilon)[:, None] * norm_gain[None, :]
    ).astype(jnp.bfloat16)
    expert_ids = jnp.arange(experts, dtype=jnp.int32)
    onehot = (routes.reshape(-1)[:, None] == expert_ids[None, :]).astype(jnp.int32)
    earlier = jnp.cumsum(onehot, axis=0) - onehot
    slot_index = jnp.sum(earlier * onehot, axis=1).reshape(tok_rows, 2)
    place_index = routes * capacity + slot_index
    positions = jnp.arange(slots_all, dtype=jnp.int32)
    first_hit = place_index[None, :, 0] == positions[:, None]
    second_hit = place_index[None, :, 1] == positions[:, None]
    dispatch = (first_hit | second_hit).astype(jnp.bfloat16)
    outgoing = (
        jnp.dot(dispatch, normed, preferred_element_type=jnp.float32)
        .astype(jnp.bfloat16)
        .reshape(experts, capacity, slice_width)
    )
    incoming = lax.all_to_all(outgoing, "expert", split_axis=0, concat_axis=0, tiled=True)
    pieces = lax.all_gather(incoming[None], ("seq", "tensor"), axis=0, tiled=True)
    rows = (
        pieces.reshape(n_seq, n_tensor, slots_all, slice_width)
        .transpose(0, 2, 1, 3)
        .reshape(n_seq * slots_all, full_width)
    )
    gate = jnp.dot(rows, w_gate[0], preferred_element_type=jnp.float32)
    up = jnp.dot(rows, w_up[0], preferred_element_type=jnp.float32)
    hidden = (jax.nn.silu(gate) * up).astype(jnp.bfloat16)
    partial = jnp.dot(hidden, w_down[0], preferred_element_type=jnp.float32).astype(jnp.bfloat16)
    blocks = (
        partial.reshape(n_seq, slots_all, n_tensor, slice_width)
        .transpose(0, 2, 1, 3)
        .reshape(n_seq * n_tensor * slots_all, slice_width)
    )
    expert_out = lax.psum_scatter(blocks, ("seq", "tensor"), scatter_dimension=0, tiled=True)
    outgoing_back = expert_out.astype(jnp.bfloat16).reshape(experts, capacity, slice_width)
    returned = lax.all_to_all(outgoing_back, "expert", split_axis=0, concat_axis=0, tiled=True)
    combine_matrix = route_weights[:, 0:1] * (place_index[:, 0:1] == positions[None, :]).astype(
        jnp.float32
    )
    combine_matrix = combine_matrix + route_weights[:, 1:2] * (
        place_index[:, 1:2] == positions[None, :]
    ).astype(jnp.float32)
    mixed_rows = jnp.dot(
        combine_matrix,
        returned.reshape(slots_all, slice_width).astype(jnp.float32),
        precision=lax.Precision.HIGHEST,
    )
    residual = (token_float + mixed_rows).astype(jnp.bfloat16)
    residual_float = residual.astype(jnp.float32)
    second_squares = lax.psum(jnp.sum(residual_float * residual_float, axis=1), "tensor")
    final_rows = (
        residual_float
        * lax.rsqrt(second_squares / full_width + epsilon)[:, None]
        * final_gain[None, :]
    ).astype(jnp.bfloat16)
    final_pieces = lax.all_gather(final_rows[None], ("expert", "tensor"), axis=0, tiled=True)
    all_rows = (
        final_pieces.reshape(n_expert, n_tensor, tok_rows, slice_width)
        .transpose(0, 2, 1, 3)
        .reshape(n_expert * tok_rows, full_width)
    )
    logits = jnp.dot(all_rows, head_weight, preferred_element_type=jnp.float32)
    vocab_start = (lax.axis_index("expert") * n_tensor + lax.axis_index("tensor")) * vocab_part
    local_top = jnp.max(logits, axis=1)
    local_total = jnp.sum(jnp.exp(logits - local_top[:, None]), axis=1)
    target_hit = targets[:, None] - vocab_start == jnp.arange(vocab_part, dtype=jnp.int32)[None, :]
    target_logit = jnp.sum(jnp.where(target_hit, logits, jnp.zeros_like(logits)), axis=1)
    own_rows = tok_rows // n_tensor
    terms = jnp.stack([local_top, local_total, target_logit])
    terms = merge_terms(lax.all_gather(terms, "expert"))
    terms = lax.dynamic_slice_in_dim(terms, lax.axis_index("expert") * tok_rows, tok_rows, 1)
    terms = merge_terms(lax.all_gather(terms, "tensor"))
    loss_all = terms[0] + jnp.log(terms[1]) - terms[2]
    return lax.dynamic_slice_in_dim(loss_all, lax.axis_index("tensor") * own_rows, own_rows)


def solution(mesh):
    return jax.shard_map(
        on_device,
        mesh=mesh,
        in_specs=(
            P(("seq", "expert"), "tensor"),
            P(("seq", "expert"), None),
            P(("seq", "expert"), None),
            P("tensor"),
            P("tensor"),
            P("expert", None, ("seq", "tensor")),
            P("expert", None, ("seq", "tensor")),
            P("expert", ("seq", "tensor"), None),
            P(None, ("expert", "tensor")),
            P("seq"),
        ),
        out_specs=P(("seq", "expert", "tensor")),
        check_vma=False,
    )
```

```python
import functools
import jax
import jax.numpy as jnp
from jax import lax
from jax.experimental import pallas as pl
from jax.experimental.pallas import tpu as pltpu
from jax.sharding import PartitionSpec as P

epsilon = 1e-05
MESH = pl.DeviceIdType.MESH
COLOR_ROWS = ((0, 48), (48, 48), (96, 32))
AXES = "xyz"


def place():
    e = lax.axis_index("expert")
    t = lax.axis_index("tensor")
    return {"x": e % 4, "y": t // 2, "z": (e // 4) * 2 + t % 2}


def device_at(pos):
    z = pos["z"]
    return (lax.axis_index("seq"), (z // 2) * 4 + pos["x"], pos["y"] * 2 + z % 2)


def moved(pos, axis, by):
    out = dict(pos)
    out[axis] = (pos[axis] + by + 4) % 4
    return out


def tensor_peer(k):
    return (lax.axis_index("seq"), lax.axis_index("expert"), (lax.axis_index("tensor") + k) % 8)


def expert_peer(k):
    return (lax.axis_index("seq"), (lax.axis_index("expert") + k) % 8, lax.axis_index("tensor"))


def remote(src, dst, send, recv, dev):
    return pltpu.make_async_remote_copy(
        src_ref=src, dst_ref=dst, send_sem=send, recv_sem=recv, device_id=dev, device_id_type=MESH
    )


def greet(peers):
    barrier = pltpu.get_barrier_semaphore()
    for dev in peers:
        pl.semaphore_signal(barrier, inc=1, device_id=dev, device_id_type=MESH)
    pl.semaphore_wait(barrier, len(peers))


def region(buf, full, pos, rows, cols):
    z = pos["z"]
    zh = pl.ds(0, 2) if "z" in full else z // 2
    zl = pl.ds(0, 2) if "z" in full else z % 2
    x = pl.ds(0, 4) if "x" in full else pos["x"]
    y = pl.ds(0, 4) if "y" in full else pos["y"]
    return buf.at[zh, x, y, zl, pl.ds(rows[0], rows[1]), pl.ds(cols[0], cols[1])]


def ring_gather(buf, send, recv):
    me = place()
    every = (0, 512)
    halves = ((0, 256), (256, 256))
    copies = []
    for phase in range(3):
        plans = []
        for color in range(3):
            axis = AXES[(color + phase) % 3]
            full = [AXES[(color + p) % 3] for p in range(phase)]
            plans.append((color, axis, full, COLOR_ROWS[color]))
        first = {}
        for color, axis, full, rows in plans:
            here = region(buf, full, me, rows, every)
            for side, by in ((0, 1), (1, -1)):
                c = remote(
                    here, here, send.at[color, phase, side], recv.at[color, phase, side],
                    device_at(moved(me, axis, by)),
                )
                c.start()
                first[color, side] = c
        second = {}
        for color, axis, full, rows in plans:
            for side, by in ((0, 1), (1, -1)):
                first[color, side].wait_recv()
                came = region(buf, full, moved(me, axis, -by), rows, halves[side])
                c = remote(
                    came, came, send.at[color, phase, 2 + side], recv.at[color, phase, 2 + side],
                    device_at(moved(me, axis, by)),
                )
                c.start()
                second[color, side] = c
        for key in second:
            second[key].wait_recv()
        copies += list(first.values()) + list(second.values())
    for c in copies:
        c.wait_send()


def swap_small(buf, mine, peer, send, recv):
    copies = []
    for k in range(1, 8):
        src, dst = mine(k)
        c = remote(src, dst, send.at[k - 1], recv.at[k - 1], peer(k))
        c.start()
        copies.append(c)
    for c in copies:
        c.wait_recv()
    return copies


def merge_stats(buf):
    tops = [buf[i, 0:1, :] for i in range(8)]
    top = functools.reduce(jnp.maximum, tops)
    total = sum(buf[i, 1:2, :] * jnp.exp(buf[i, 0:1, :] - top) for i in range(8))
    target = sum(buf[i, 2:3, :] for i in range(8))
    return top, total, target


def head_body(
    res_ref, gain_ref, head_ref, tgt_ref, out_ref,
    buf, acc, sq, stats, join_e, join_t,
    send, recv, sq_send, sq_recv, je_send, je_recv, jt_send, jt_recv,
):
    me = place()
    e = lax.axis_index("expert")
    t = lax.axis_index("tensor")
    cross = 1 - 2 * (me["z"] % 2)
    greet(
        [tensor_peer(k) for k in range(1, 8)]
        + [expert_peer(k) for k in range(1, 8)]
        + [device_at(moved(me, "z", -cross))]
    )
    x = res_ref[...].astype(jnp.float32)
    part = jnp.sum(x * x, axis=1, keepdims=True)
    sq[t] = jnp.broadcast_to(part, (128, 128)).T[0:8]
    small = swap_small(sq, lambda k: (sq.at[t], sq.at[t]), tensor_peer, sq_send, sq_recv)
    squares = sum(sq[i] for i in range(8))[0:1]
    scale = lax.rsqrt(squares / 4096.0 + epsilon)
    column = jnp.broadcast_to(scale, (128, 128)).T
    rows = (x * column[:, 0:1] * gain_ref[...]).astype(jnp.bfloat16)
    buf[me["z"] // 2, me["x"], me["y"], me["z"] % 2] = rows
    ring_gather(buf, send, recv)

    acc[...] = jnp.zeros_like(acc)

    @pl.loop(0, 8)
    def _(k):
        piece = buf[:, :, k // 2, k % 2].reshape(1024, 512)
        acc[...] += jnp.dot(
            piece, head_ref[pl.ds(k * 512, 512), :], preferred_element_type=jnp.float32
        )

    start = (e * 8 + t) * 500

    @pl.loop(0, 8)
    def _(i):
        block = acc[pl.ds(i * 128, 128), :]
        top = jnp.max(block, axis=1, keepdims=True)
        total = jnp.sum(jnp.exp(block - top), axis=1, keepdims=True)
        ids = lax.broadcasted_iota(jnp.int32, block.shape, 1) + start
        hit = tgt_ref[pl.ds(i * 128, 128), :] == ids
        target = jnp.sum(jnp.where(hit, block, 0.0), axis=1, keepdims=True)
        lane = lax.broadcasted_iota(jnp.int32, (128, 128), 1)
        three = jnp.where(lane == 0, top, jnp.where(lane == 1, total, target))
        stats[i] = three.T[0:8]

    join_e[e] = stats[e]
    small += swap_small(
        join_e, lambda k: (stats.at[(e + k) % 8], join_e.at[e]), expert_peer, je_send, je_recv
    )
    top, total, target = merge_stats(join_e)
    join_t[t, 0:1] = top
    join_t[t, 1:2] = total
    join_t[t, 2:3] = target
    join_t[t, 3:8] = jnp.zeros((5, 128), jnp.float32)
    small += swap_small(
        join_t, lambda k: (join_t.at[t], join_t.at[t]), tensor_peer, jt_send, jt_recv
    )
    top, total, target = merge_stats(join_t)
    out_ref[...] = jnp.broadcast_to(top + jnp.log(total) - target, out_ref.shape)
    for c in small:
        c.wait_send()


def head_loss(residual, gain, head_weight, targets):
    vmem = pl.BlockSpec(memory_space=pltpu.VMEM)
    sem = pltpu.SemaphoreType.DMA
    return pl.pallas_call(
        head_body,
        out_shape=jax.ShapeDtypeStruct((8, 128), jnp.float32),
        in_specs=[vmem] * 4,
        out_specs=vmem,
        scratch_shapes=[
            pltpu.VMEM((2, 4, 4, 2, 128, 512), jnp.bfloat16),
            pltpu.VMEM((1024, 500), jnp.float32),
            pltpu.VMEM((8, 8, 128), jnp.float32),
            pltpu.VMEM((8, 8, 128), jnp.float32),
            pltpu.VMEM((8, 8, 128), jnp.float32),
            pltpu.VMEM((8, 8, 128), jnp.float32),
            sem((3, 3, 4)), sem((3, 3, 4)),
            sem((7,)), sem((7,)), sem((7,)), sem((7,)), sem((7,)), sem((7,)),
        ],
        compiler_params=pltpu.CompilerParams(
            collective_id=0, has_side_effects=True, vmem_limit_bytes=40 * 2**20
        ),
        name="head_loss",
    )(residual, gain.reshape(1, 512), head_weight, targets.reshape(1024, 1))


def on_device(
    tokens, routes, route_weights, norm_gain, final_gain, w_gate, w_up, w_down, head_weight, targets
):
    tok_rows, slice_width = tokens.shape
    n_seq = lax.axis_size("seq")
    n_expert = lax.axis_size("expert")
    n_tensor = lax.axis_size("tensor")
    full_width = slice_width * n_tensor
    experts = w_gate.shape[0] * n_expert
    capacity = 4 * tok_rows // experts
    slots_all = experts * capacity
    token_float = tokens.astype(jnp.float32)
    first_squares = lax.psum(jnp.sum(token_float * token_float, axis=1), "tensor")
    normed = (
        token_float * lax.rsqrt(first_squares / full_width + epsilon)[:, None] * norm_gain[None, :]
    ).astype(jnp.bfloat16)
    expert_ids = jnp.arange(experts, dtype=jnp.int32)
    onehot = (routes.reshape(-1)[:, None] == expert_ids[None, :]).astype(jnp.int32)
    earlier = jnp.cumsum(onehot, axis=0) - onehot
    slot_index = jnp.sum(earlier * onehot, axis=1).reshape(tok_rows, 2)
    place_index = routes * capacity + slot_index
    positions = jnp.arange(slots_all, dtype=jnp.int32)
    first_hit = place_index[None, :, 0] == positions[:, None]
    second_hit = place_index[None, :, 1] == positions[:, None]
    dispatch = (first_hit | second_hit).astype(jnp.bfloat16)
    outgoing = (
        jnp.dot(dispatch, normed, preferred_element_type=jnp.float32)
        .astype(jnp.bfloat16)
        .reshape(experts, capacity, slice_width)
    )
    incoming = lax.all_to_all(outgoing, "expert", split_axis=0, concat_axis=0, tiled=True)
    pieces = lax.all_gather(incoming[None], ("seq", "tensor"), axis=0, tiled=True)
    rows = (
        pieces.reshape(n_seq, n_tensor, slots_all, slice_width)
        .transpose(0, 2, 1, 3)
        .reshape(n_seq * slots_all, full_width)
    )
    gate = jnp.dot(rows, w_gate[0], preferred_element_type=jnp.float32)
    up = jnp.dot(rows, w_up[0], preferred_element_type=jnp.float32)
    hidden = (jax.nn.silu(gate) * up).astype(jnp.bfloat16)
    partial = jnp.dot(hidden, w_down[0], preferred_element_type=jnp.float32).astype(jnp.bfloat16)
    blocks = (
        partial.reshape(n_seq, slots_all, n_tensor, slice_width)
        .transpose(0, 2, 1, 3)
        .reshape(n_seq * n_tensor * slots_all, slice_width)
    )
    expert_out = lax.psum_scatter(blocks, ("seq", "tensor"), scatter_dimension=0, tiled=True)
    outgoing_back = expert_out.astype(jnp.bfloat16).reshape(experts, capacity, slice_width)
    returned = lax.all_to_all(outgoing_back, "expert", split_axis=0, concat_axis=0, tiled=True)
    combine_matrix = route_weights[:, 0:1] * (place_index[:, 0:1] == positions[None, :]).astype(
        jnp.float32
    )
    combine_matrix = combine_matrix + route_weights[:, 1:2] * (
        place_index[:, 1:2] == positions[None, :]
    ).astype(jnp.float32)
    mixed_rows = jnp.dot(
        combine_matrix,
        returned.reshape(slots_all, slice_width).astype(jnp.float32),
        precision=lax.Precision.HIGHEST,
    )
    residual = (token_float + mixed_rows).astype(jnp.bfloat16)
    loss = head_loss(residual, final_gain, head_weight, targets)[0]
    own_rows = tok_rows // n_tensor
    return lax.dynamic_slice_in_dim(loss, lax.axis_index("tensor") * own_rows, own_rows)


def solution(mesh):
    return jax.shard_map(
        on_device,
        mesh=mesh,
        in_specs=(
            P(("seq", "expert"), "tensor"),
            P(("seq", "expert"), None),
            P(("seq", "expert"), None),
            P("tensor"),
            P("tensor"),
            P("expert", None, ("seq", "tensor")),
            P("expert", None, ("seq", "tensor")),
            P("expert", ("seq", "tensor"), None),
            P(None, ("expert", "tensor")),
            P("seq"),
        ),
        out_specs=P(("seq", "expert", "tensor")),
        check_vma=False,
    )
```

```python
import functools
import jax
import jax.numpy as jnp
from jax import lax
from jax.experimental import pallas as pl
from jax.experimental.pallas import tpu as pltpu
from jax.sharding import PartitionSpec as P

epsilon = 1e-05
MESH = pl.DeviceIdType.MESH
COLOR_ROWS = ((0, 48), (48, 48), (96, 32))
AXES = "xyz"


def place():
    e = lax.axis_index("expert")
    t = lax.axis_index("tensor")
    return {"x": e % 4, "y": t // 2, "z": (e // 4) * 2 + t % 2}


def device_at(pos):
    z = pos["z"]
    return (lax.axis_index("seq"), (z // 2) * 4 + pos["x"], pos["y"] * 2 + z % 2)


def moved(pos, axis, by):
    out = dict(pos)
    out[axis] = (pos[axis] + by + 4) % 4
    return out


def tensor_peer(k):
    return (lax.axis_index("seq"), lax.axis_index("expert"), (lax.axis_index("tensor") + k) % 8)


def expert_peer(k):
    return (lax.axis_index("seq"), (lax.axis_index("expert") + k) % 8, lax.axis_index("tensor"))


def remote(src, dst, send, recv, dev):
    return pltpu.make_async_remote_copy(
        src_ref=src, dst_ref=dst, send_sem=send, recv_sem=recv, device_id=dev, device_id_type=MESH
    )


def greet(peers):
    barrier = pltpu.get_barrier_semaphore()
    for dev in peers:
        pl.semaphore_signal(barrier, inc=1, device_id=dev, device_id_type=MESH)
    pl.semaphore_wait(barrier, len(peers))


def region(buf, full, pos, rows, cols):
    z = pos["z"]
    zh = pl.ds(0, 2) if "z" in full else z // 2
    zl = pl.ds(0, 2) if "z" in full else z % 2
    x = pl.ds(0, 4) if "x" in full else pos["x"]
    y = pl.ds(0, 4) if "y" in full else pos["y"]
    return buf.at[zh, x, y, zl, pl.ds(rows[0], rows[1]), pl.ds(cols[0], cols[1])]


def ring_gather(buf, send, recv):
    me = place()
    every = (0, 512)
    halves = ((0, 256), (256, 256))
    copies = []
    for phase in range(3):
        plans = []
        for color in range(3):
            axis = AXES[(color + phase) % 3]
            full = [AXES[(color + p) % 3] for p in range(phase)]
            plans.append((color, axis, full, COLOR_ROWS[color]))
        first = {}
        for color, axis, full, rows in plans:
            here = region(buf, full, me, rows, every)
            for side, by in ((0, 1), (1, -1)):
                c = remote(
                    here, here, send.at[color, phase, side], recv.at[color, phase, side],
                    device_at(moved(me, axis, by)),
                )
                c.start()
                first[color, side] = c
        second = {}
        for color, axis, full, rows in plans:
            for side, by in ((0, 1), (1, -1)):
                first[color, side].wait_recv()
                came = region(buf, full, moved(me, axis, -by), rows, halves[side])
                c = remote(
                    came, came, send.at[color, phase, 2 + side], recv.at[color, phase, 2 + side],
                    device_at(moved(me, axis, by)),
                )
                c.start()
                second[color, side] = c
        for key in second:
            second[key].wait_recv()
        copies += list(first.values()) + list(second.values())
    for c in copies:
        c.wait_send()


def swap_small(buf, mine, peer, send, recv):
    copies = []
    for k in range(1, 8):
        src, dst = mine(k)
        c = remote(src, dst, send.at[k - 1], recv.at[k - 1], peer(k))
        c.start()
        copies.append(c)
    for c in copies:
        c.wait_recv()
    return copies


def merge_stats(buf):
    tops = [buf[i, 0:1, :] for i in range(8)]
    top = functools.reduce(jnp.maximum, tops)
    total = sum(buf[i, 1:2, :] * jnp.exp(buf[i, 0:1, :] - top) for i in range(8))
    target = sum(buf[i, 2:3, :] for i in range(8))
    return top, total, target


def head_body(
    res_ref, gain_ref, head_ref, tgt_ref, out_ref,
    buf, acc, sq, stats, join_e, join_t,
    send, recv, sq_send, sq_recv, je_send, je_recv, jt_send, jt_recv,
):
    me = place()
    e = lax.axis_index("expert")
    t = lax.axis_index("tensor")
    cross = 1 - 2 * (me["z"] % 2)
    greet(
        [tensor_peer(k) for k in range(1, 8)]
        + [expert_peer(k) for k in range(1, 8)]
        + [device_at(moved(me, "z", -cross))]
    )
    x = res_ref[...].astype(jnp.float32)
    part = jnp.sum(x * x, axis=1, keepdims=True)
    sq[t] = jnp.broadcast_to(part, (128, 128)).T[0:8]
    small = swap_small(sq, lambda k: (sq.at[t], sq.at[t]), tensor_peer, sq_send, sq_recv)
    squares = sum(sq[i] for i in range(8))[0:1]
    scale = lax.rsqrt(squares / 4096.0 + epsilon)
    column = jnp.broadcast_to(scale, (128, 128)).T
    rows = (x * column[:, 0:1] * gain_ref[...]).astype(jnp.bfloat16)
    buf[me["z"] // 2, me["x"], me["y"], me["z"] % 2] = rows
    ring_gather(buf, send, recv)

    acc[...] = jnp.zeros_like(acc)

    @pl.loop(0, 8)
    def _(k):
        piece = buf[:, :, k // 2, k % 2].reshape(1024, 512)
        acc[...] += jnp.dot(
            piece, head_ref[pl.ds(k * 512, 512), :], preferred_element_type=jnp.float32
        )

    start = (e * 8 + t) * 500

    @pl.loop(0, 8)
    def _(i):
        block = acc[pl.ds(i * 128, 128), :]
        top = jnp.max(block, axis=1, keepdims=True)
        total = jnp.sum(jnp.exp(block - top), axis=1, keepdims=True)
        ids = lax.broadcasted_iota(jnp.int32, block.shape, 1) + start
        hit = tgt_ref[pl.ds(i * 128, 128), :] == ids
        target = jnp.sum(jnp.where(hit, block, 0.0), axis=1, keepdims=True)
        lane = lax.broadcasted_iota(jnp.int32, (128, 128), 1)
        three = jnp.where(lane == 0, top, jnp.where(lane == 1, total, target))
        stats[i] = three.T[0:8]

    join_e[e] = stats[e]
    small += swap_small(
        join_e, lambda k: (stats.at[(e + k) % 8], join_e.at[e]), expert_peer, je_send, je_recv
    )
    top, total, target = merge_stats(join_e)
    join_t[t, 0:1] = top
    join_t[t, 1:2] = total
    join_t[t, 2:3] = target
    join_t[t, 3:8] = jnp.zeros((5, 128), jnp.float32)
    small += swap_small(
        join_t, lambda k: (join_t.at[t], join_t.at[t]), tensor_peer, jt_send, jt_recv
    )
    top, total, target = merge_stats(join_t)
    out_ref[...] = jnp.broadcast_to(top + jnp.log(total) - target, out_ref.shape)
    for c in small:
        c.wait_send()


def head_loss(residual, gain, head_weight, targets):
    vmem = pl.BlockSpec(memory_space=pltpu.VMEM)
    sem = pltpu.SemaphoreType.DMA
    return pl.pallas_call(
        head_body,
        out_shape=jax.ShapeDtypeStruct((8, 128), jnp.float32),
        in_specs=[vmem] * 4,
        out_specs=vmem,
        scratch_shapes=[
            pltpu.VMEM((2, 4, 4, 2, 128, 512), jnp.bfloat16),
            pltpu.VMEM((1024, 500), jnp.float32),
            pltpu.VMEM((8, 8, 128), jnp.float32),
            pltpu.VMEM((8, 8, 128), jnp.float32),
            pltpu.VMEM((8, 8, 128), jnp.float32),
            pltpu.VMEM((8, 8, 128), jnp.float32),
            sem((3, 3, 4)), sem((3, 3, 4)),
            sem((7,)), sem((7,)), sem((7,)), sem((7,)), sem((7,)), sem((7,)),
        ],
        compiler_params=pltpu.CompilerParams(
            collective_id=0, has_side_effects=True, vmem_limit_bytes=40 * 2**20
        ),
        name="head_loss",
    )(residual, gain.reshape(1, 512), head_weight, targets.reshape(1024, 1))


CHUNKS = 2
CHUNK_ROWS = 256
Z_FIRST = (0, 144)
Y_FIRST = (144, 112)
HIDDEN_TILES = ((0, 256), (256, 256), (512, 256), (768, 128))


class Lane:
    def __init__(self, send, recv, chunk):
        self.send, self.recv, self.chunk, self.used, self.copies = send, recv, chunk, 0, []

    def start(self, src, dst, dev):
        c = remote(
            src, dst, self.send.at[self.chunk, self.used], self.recv.at[self.chunk, self.used], dev
        )
        self.used += 1
        c.start()
        self.copies.append(c)
        return c

    def finish(self):
        for c in self.copies:
            c.wait_send()


def expert_body(
    tok_ref, gain_ref, routes_ref, weights_ref, wg_hbm, wu_hbm, wd_hbm, out_ref,
    wg, wu, wd, sent, X, hidden, part, twin, ra1, ra2, ra3, rb1, rb2, rb3, back, sq,
    w_sem, sq_send, sq_recv, g_send, g_recv, r_send, r_recv,
):
    me = place()
    s = lax.axis_index("seq")
    e = lax.axis_index("expert")
    t = lax.axis_index("tensor")
    y, zl = me["y"], t % 2
    f32, bf16 = jnp.float32, jnp.bfloat16
    loads = [
        pltpu.make_async_copy(src.at[0], dst, w_sem.at[i])
        for i, (src, dst) in enumerate(((wg_hbm, wg), (wu_hbm, wu), (wd_hbm, wd)))
    ]
    for c in loads:
        c.start()
    twin_dev = (1 - s, e, t)
    pair_dev = (s, e, y * 2 + 1 - zl)

    def y_dev(by):
        return (s, e, ((y + by + 4) % 4) * 2 + zl)

    def at_y(by):
        return (y + by + 4) % 4

    greet(
        [tensor_peer(k) for k in range(1, 8)]
        + [expert_peer(k) for k in range(1, 8)]
        + [twin_dev]
    )
    x = tok_ref[...].astype(f32)
    sq[t] = jnp.broadcast_to(jnp.sum(x * x, axis=1, keepdims=True), (128, 128)).T[0:8]
    small = swap_small(sq, lambda k: (sq.at[t], sq.at[t]), tensor_peer, sq_send, sq_recv)
    squares = sum(sq[i] for i in range(8))[0:1]
    column = jnp.broadcast_to(lax.rsqrt(squares / 4096.0 + epsilon), (128, 128)).T
    normed = (x * column[:, 0:1] * gain_ref[...]).astype(bf16)
    names = [routes_ref[j : j + 1, :] for j in range(2)]
    ids = lax.broadcasted_iota(jnp.int32, (8, 128), 0)
    named = ((names[0] == ids) | (names[1] == ids)).astype(f32)
    lower = (
        lax.broadcasted_iota(jnp.int32, (128, 128), 0)
        < lax.broadcasted_iota(jnp.int32, (128, 128), 1)
    ).astype(f32)
    earlier = jnp.dot(named, lower, preferred_element_type=f32)
    slot_ids = lax.broadcasted_iota(jnp.int32, (32, 128), 0).astype(f32)

    def selection(j, chunk, i):
        own = earlier[i : i + 1] == slot_ids + 32.0 * chunk
        if j is None:
            hit = named[i : i + 1] > 0.5
        else:
            hit = names[j] == i
        return jnp.where(own & hit, 1.0, 0.0)

    for chunk in range(CHUNKS):
        pick = jnp.concatenate([selection(None, chunk, i) for i in range(8)], axis=0)
        sent[chunk] = jnp.dot(
            pick.astype(bf16), normed, preferred_element_type=f32
        ).astype(bf16)

    def cols(first, n):
        return pl.ds(pl.multiple_of(first, 256), n)

    def rows_of(i):
        return pl.ds(pl.multiple_of(i * 32, 32), 32)

    lanes = [Lane(g_send, g_recv, c) for c in range(CHUNKS)]
    sums = [Lane(r_send, r_recv, c) for c in range(CHUNKS)]
    own_cols = cols(t * 512, 512)
    arrivals = []
    for chunk in range(CHUNKS):
        X[chunk, s, rows_of(e), own_cols] = sent[chunk, rows_of(e), :]
        arrivals.append([
            lanes[chunk].start(
                sent.at[chunk, rows_of((e + k) % 8)],
                X.at[chunk, s, rows_of(e), own_cols],
                expert_peer(k),
            )
            for k in range(1, 8)
        ])

    def gather(chunk):
        lane = lanes[chunk]

        def view(rows, first, n):
            return X.at[chunk, s, pl.ds(*rows), cols(first, n)]

        def put(rows, first, n, dev):
            v = view(rows, first, n)
            return lane.start(v, v, dev)

        for c in arrivals[chunk]:
            c.wait_recv()
        az = put(Z_FIRST, t * 512, 512, pair_dev)
        by = [put(Y_FIRST, t * 512, 512, y_dev(d)) for d in (1, -1)]
        bz = [put(Y_FIRST, t * 512, 512, pair_dev)]
        yield
        az.wait_recv()
        ay = [put(Z_FIRST, y * 1024, 1024, y_dev(d)) for d in (1, -1)]
        twins = [put(Z_FIRST, y * 1024, 1024, twin_dev)]
        bh = []
        for side, d in ((0, 1), (1, -1)):
            by[side].wait_recv()
            first = (at_y(-d) * 2 + zl) * 512
            bh.append(put(Y_FIRST, first + 256 * side, 256, y_dev(d)))
            bz.append(put(Y_FIRST, first, 512, pair_dev))
        yield
        ah = []
        for side, d in ((0, 1), (1, -1)):
            ay[side].wait_recv()
            first = at_y(-d) * 1024
            ah.append(put(Z_FIRST, first + 512 * side, 512, y_dev(d)))
            twins.append(put(Z_FIRST, first, 1024, twin_dev))
        for c in bh:
            c.wait_recv()
        bz.append(put(Y_FIRST, (at_y(2) * 2 + zl) * 512, 512, pair_dev))
        for i, d in enumerate((0, -1, 1)):
            bz[i].wait_recv()
            twins.append(put(Y_FIRST, at_y(d) * 1024, 1024, twin_dev))
        yield
        for c in ah:
            c.wait_recv()
        twins.append(put(Z_FIRST, at_y(2) * 1024, 1024, twin_dev))
        bz[3].wait_recv()
        twins.append(put(Y_FIRST, at_y(2) * 1024, 1024, twin_dev))
        yield
        for c in twins:
            c.wait_recv()

    pending = [[] for _ in range(CHUNKS)]

    def compute(chunk):
        def up_step(first, n):
            def step():
                rows = X[chunk].reshape(2 * CHUNK_ROWS, 4096)
                gate = jnp.dot(rows, wg[:, first : first + n], preferred_element_type=f32)
                up = jnp.dot(rows, wu[:, first : first + n], preferred_element_type=f32)
                hidden[:, first : first + n] = (gate / (1.0 + jnp.exp(-gate)) * up).astype(bf16)
            return step

        def down_step(k):
            def step():
                first = k * 512
                done = jnp.dot(hidden[...], wd[:, first : first + 512], preferred_element_type=f32)
                part[chunk, :, :, first : first + 512] = done.astype(bf16).reshape(
                    2, CHUNK_ROWS, 512
                )
                pending[chunk].append(
                    sums[chunk].start(
                        part.at[chunk, 1 - s, :, pl.ds(first, 512)],
                        twin.at[chunk, :, pl.ds(first, 512)],
                        twin_dev,
                    )
                )
            return step

        return [up_step(*tile) for tile in HIDDEN_TILES] + [down_step(k) for k in range(8)]

    def reduce(chunk):
        lane = sums[chunk]

        def add(rows, first, n, *others):
            block = part[chunk, s, pl.ds(*rows), cols(first, n)].astype(f32)
            for o in others:
                block = block + o.astype(f32)
            part[chunk, s, pl.ds(*rows), cols(first, n)] = block.astype(bf16)

        def put(rows, first, n, dst, dev):
            return lane.start(part.at[chunk, s, pl.ds(*rows), cols(first, n)], dst, dev)

        for k in range(8):
            pending[chunk][k].wait_recv()
            first = k * 512
            part[chunk, s, :, first : first + 512] = (
                part[chunk, s, :, first : first + 512].astype(f32)
                + twin[chunk, :, first : first + 512].astype(f32)
            ).astype(bf16)
        a1 = [
            put(Z_FIRST, at_y(2) * 1024 + 512 * h, 512, ra1.at[chunk, h], y_dev(d))
            for h, d in ((0, -1), (1, 1))
        ]
        b1 = [
            put(Y_FIRST, (at_y(d) * 2 + 1 - zl) * 512, 512, rb1.at[chunk, i], pair_dev)
            for i, d in enumerate((2, 1, -1, 0))
        ]
        yield
        b1[0].wait_recv()
        add(Y_FIRST, (at_y(2) * 2 + zl) * 512, 512, rb1[chunk, 0])
        b2 = [
            put(Y_FIRST, (at_y(2) * 2 + zl) * 512 + 256 * h, 256, rb2.at[chunk, h], y_dev(d))
            for h, d in ((0, -1), (1, 1))
        ]
        a2 = []
        for h, d in ((0, -1), (1, 1)):
            a1[h].wait_recv()
            add(Z_FIRST, at_y(d) * 1024 + 512 * h, 512, ra1[chunk, h])
            a2.append(put(Z_FIRST, at_y(d) * 1024, 1024, ra2.at[chunk, h], y_dev(d)))
        yield
        for i, d in ((1, 1), (2, -1), (3, 0)):
            b1[i].wait_recv()
            add(Y_FIRST, (at_y(d) * 2 + zl) * 512, 512, rb1[chunk, i])
        b3 = []
        for h, d in ((0, -1), (1, 1)):
            b2[h].wait_recv()
            first = (at_y(d) * 2 + zl) * 512
            add(Y_FIRST, first + 256 * h, 256, rb2[chunk, h])
            b3.append(put(Y_FIRST, first, 512, rb3.at[chunk, h], y_dev(d)))
        yield
        for c in a2:
            c.wait_recv()
        add(Z_FIRST, y * 1024, 1024, ra2[chunk, 0], ra2[chunk, 1])
        a3 = put(Z_FIRST, (y * 2 + 1 - zl) * 512, 512, ra3.at[chunk], pair_dev)
        for c in b3:
            c.wait_recv()
        add(Y_FIRST, t * 512, 512, rb3[chunk, 0], rb3[chunk, 1])
        yield
        a3.wait_recv()
        add(Z_FIRST, t * 512, 512, ra3[chunk])
        back[chunk, rows_of(e), :] = part[chunk, s, rows_of(e), own_cols]
        homes = [
            lane.start(
                part.at[chunk, s, rows_of((e + k) % 8), own_cols],
                back.at[chunk, rows_of(e)],
                expert_peer(k),
            )
            for k in range(1, 8)
        ]
        yield
        for c in homes:
            c.wait_recv()

    def drain(moves):
        for _ in moves:
            pass

    def weave(steps, moves, every):
        for i, step in enumerate(steps):
            step()
            if (i + 1) % every == 0:
                next(moves, None)
        drain(moves)

    first_moves, later_moves = gather(0), gather(1)
    for _ in range(4):
        next(first_moves, None)
    next(later_moves, None)
    drain(first_moves)
    for c in loads:
        c.wait()
    weave(compute(0), later_moves, 1)
    back_moves = reduce(0)
    next(back_moves, None)
    weave(compute(1), back_moves, 1)
    drain(reduce(1))

    mixed = jnp.zeros((128, 512), f32)
    for j in range(2):
        total = jnp.zeros((128, 512), f32)
        for chunk in range(CHUNKS):
            pick = jnp.concatenate([selection(j, chunk, i) for i in range(8)], axis=0)
            total = total + lax.dot_general(
                pick.T.astype(bf16), back[chunk], (((1,), (0,)), ((), ())),
                preferred_element_type=f32,
            )
        mixed = mixed + weights_ref[:, j : j + 1] * total
    out_ref[...] = (x + mixed).astype(bf16)
    for c in small:
        c.wait_send()
    for lane in lanes + sums:
        lane.finish()


def expert_layer(tokens, gain, routes, route_weights, w_gate, w_up, w_down):
    vmem = pl.BlockSpec(memory_space=pltpu.VMEM)
    hbm = pl.BlockSpec(memory_space=pl.ANY)
    sem = pltpu.SemaphoreType.DMA
    bf16 = jnp.bfloat16
    a, b = Z_FIRST[1], Y_FIRST[1]
    return pl.pallas_call(
        expert_body,
        out_shape=jax.ShapeDtypeStruct((128, 512), bf16),
        in_specs=[vmem] * 4 + [hbm] * 3,
        out_specs=vmem,
        scratch_shapes=[
            pltpu.VMEM((4096, 896), bf16),
            pltpu.VMEM((4096, 896), bf16),
            pltpu.VMEM((896, 4096), bf16),
            pltpu.VMEM((CHUNKS, CHUNK_ROWS, 512), bf16),
            pltpu.VMEM((CHUNKS, 2, CHUNK_ROWS, 4096), bf16),
            pltpu.VMEM((2 * CHUNK_ROWS, 896), bf16),
            pltpu.VMEM((CHUNKS, 2, CHUNK_ROWS, 4096), bf16),
            pltpu.VMEM((CHUNKS, CHUNK_ROWS, 4096), bf16),
            pltpu.VMEM((CHUNKS, 2, a, 512), bf16),
            pltpu.VMEM((CHUNKS, 2, a, 1024), bf16),
            pltpu.VMEM((CHUNKS, a, 512), bf16),
            pltpu.VMEM((CHUNKS, 4, b, 512), bf16),
            pltpu.VMEM((CHUNKS, 2, b, 256), bf16),
            pltpu.VMEM((CHUNKS, 2, b, 512), bf16),
            pltpu.VMEM((CHUNKS, CHUNK_ROWS, 512), bf16),
            pltpu.VMEM((8, 8, 128), jnp.float32),
            sem((3,)), sem((7,)), sem((7,)),
            sem((CHUNKS, 32)), sem((CHUNKS, 32)), sem((CHUNKS, 32)), sem((CHUNKS, 32)),
        ],
        compiler_params=pltpu.CompilerParams(
            collective_id=1, has_side_effects=True, vmem_limit_bytes=62 * 2**20
        ),
        name="expert_layer",
    )(tokens, gain.reshape(1, 512), routes.T, route_weights, w_gate, w_up, w_down)


def on_device(
    tokens, routes, route_weights, norm_gain, final_gain, w_gate, w_up, w_down, head_weight, targets
):
    residual = expert_layer(tokens, norm_gain, routes, route_weights, w_gate, w_up, w_down)
    loss = head_loss(residual, final_gain, head_weight, targets)[0]
    own_rows = tokens.shape[0] // 8
    return lax.dynamic_slice_in_dim(loss, lax.axis_index("tensor") * own_rows, own_rows)


def solution(mesh):
    return jax.shard_map(
        on_device,
        mesh=mesh,
        in_specs=(
            P(("seq", "expert"), "tensor"),
            P(("seq", "expert"), None),
            P(("seq", "expert"), None),
            P("tensor"),
            P("tensor"),
            P("expert", None, ("seq", "tensor")),
            P("expert", None, ("seq", "tensor")),
            P("expert", ("seq", "tensor"), None),
            P(None, ("expert", "tensor")),
            P("seq"),
        ),
        out_specs=P(("seq", "expert", "tensor")),
        check_vma=False,
    )
```

```python
import functools
import jax
import jax.numpy as jnp
from jax import lax
from jax.experimental import pallas as pl
from jax.experimental.pallas import tpu as pltpu
from jax.sharding import PartitionSpec as P

epsilon = 1e-05
MESH = pl.DeviceIdType.MESH
COLOR_ROWS = ((0, 48), (48, 48), (96, 32))
AXES = "xyz"


def place():
    e = lax.axis_index("expert")
    t = lax.axis_index("tensor")
    return {"x": e % 4, "y": t // 2, "z": (e // 4) * 2 + t % 2}


def device_at(pos):
    z = pos["z"]
    return (lax.axis_index("seq"), (z // 2) * 4 + pos["x"], pos["y"] * 2 + z % 2)


def moved(pos, axis, by):
    out = dict(pos)
    out[axis] = (pos[axis] + by + 4) % 4
    return out


def tensor_peer(k):
    return (lax.axis_index("seq"), lax.axis_index("expert"), (lax.axis_index("tensor") + k) % 8)


def expert_peer(k):
    return (lax.axis_index("seq"), (lax.axis_index("expert") + k) % 8, lax.axis_index("tensor"))


def remote(src, dst, send, recv, dev):
    return pltpu.make_async_remote_copy(
        src_ref=src, dst_ref=dst, send_sem=send, recv_sem=recv, device_id=dev, device_id_type=MESH
    )


def greet(peers):
    barrier = pltpu.get_barrier_semaphore()
    for dev in peers:
        pl.semaphore_signal(barrier, inc=1, device_id=dev, device_id_type=MESH)


def region(buf, full, pos, rows, cols):
    z = pos["z"]
    zh = pl.ds(0, 2) if "z" in full else z // 2
    zl = pl.ds(0, 2) if "z" in full else z % 2
    x = pl.ds(0, 4) if "x" in full else pos["x"]
    y = pl.ds(0, 4) if "y" in full else pos["y"]
    return buf.at[zh, x, y, zl, pl.ds(rows[0], rows[1]), pl.ds(cols[0], cols[1])]


def ring_gather(buf, send, recv):
    me = place()
    every = (0, 512)
    halves = ((0, 256), (256, 256))
    copies = []
    for phase in range(3):
        plans = []
        for color in range(3):
            axis = AXES[(color + phase) % 3]
            full = [AXES[(color + p) % 3] for p in range(phase)]
            plans.append((color, axis, full, COLOR_ROWS[color]))
        first = {}
        for color, axis, full, rows in plans:
            here = region(buf, full, me, rows, every)
            for side, by in ((0, 1), (1, -1)):
                c = remote(
                    here, here, send.at[color, phase, side], recv.at[color, phase, side],
                    device_at(moved(me, axis, by)),
                )
                c.start()
                first[color, side] = c
        second = {}
        for color, axis, full, rows in plans:
            for side, by in ((0, 1), (1, -1)):
                first[color, side].wait_recv()
                came = region(buf, full, moved(me, axis, -by), rows, halves[side])
                c = remote(
                    came, came, send.at[color, phase, 2 + side], recv.at[color, phase, 2 + side],
                    device_at(moved(me, axis, by)),
                )
                c.start()
                second[color, side] = c
        for key in second:
            second[key].wait_recv()
        copies += list(first.values()) + list(second.values())
        yield
    for c in copies:
        c.wait_send()


def swap_small(buf, mine, peer, send, recv):
    copies = []
    for k in range(1, 8):
        src, dst = mine(k)
        c = remote(src, dst, send.at[k - 1], recv.at[k - 1], peer(k))
        c.start()
        copies.append(c)
    return copies


def arrived(copies):
    for c in copies:
        c.wait_recv()
    return copies


def squares_row(x):
    return jnp.broadcast_to(jnp.sum(x * x, axis=1, keepdims=True), (128, 128)).T[0:8]


def merge_stats(buf):
    tops = [buf[i, 0:1, :] for i in range(8)]
    top = functools.reduce(jnp.maximum, tops)
    total = sum(buf[i, 1:2, :] * jnp.exp(buf[i, 0:1, :] - top) for i in range(8))
    target = sum(buf[i, 2:3, :] for i in range(8))
    return top, total, target


def head_part(
    x, gain_ref, head_load, head_t, tgt_ref, out_ref, buf, acc, sq, stats, join_e, join_t,
    send, recv, sq_send, sq_recv, je_send, je_recv, jt_send, jt_recv, scales, sc_send, sc_recv,
):
    me = place()
    e = lax.axis_index("expert")
    t = lax.axis_index("tensor")
    sq[t] = squares_row(x)
    buf[me["z"] // 2, me["x"], me["y"], me["z"] % 2] = (x * gain_ref[...]).astype(jnp.bfloat16)
    moves = ring_gather(buf, send, recv)
    small = swap_small(sq, lambda k: (sq.at[t], sq.at[t]), tensor_peer, sq_send, sq_recv)
    next(moves)
    arrived(small)
    scales[e] = lax.rsqrt(sum(sq[i] for i in range(8)) / 4096.0 + epsilon)
    spread = swap_small(
        scales, lambda k: (scales.at[e], scales.at[e]), expert_peer, sc_send, sc_recv
    )
    next(moves)
    next(moves)
    next(moves, None)
    small += arrived(spread)

    head_load.wait()
    acc[...] = jnp.zeros_like(acc)

    @pl.loop(0, 8)
    def _(k):
        piece = buf[:, :, k // 2, k % 2].reshape(1024, 512)
        acc[...] += lax.dot_general(
            piece, head_t[:, pl.ds(pl.multiple_of(k * 512, 512), 512)], (((1,), (1,)), ((), ())),
            preferred_element_type=jnp.float32,
        )

    start = (e * 8 + t) * 500

    @pl.loop(0, 8)
    def _(i):
        column = jnp.broadcast_to(scales[i, 0:1, :], (128, 128)).T
        block = acc[pl.ds(i * 128, 128), :] * column[:, 0:1]
        top = jnp.max(block, axis=1, keepdims=True)
        total = jnp.sum(jnp.exp(block - top), axis=1, keepdims=True)
        ids = (lax.broadcasted_iota(jnp.int32, block.shape, 1) + start).astype(jnp.float32)
        wanted = jnp.broadcast_to(tgt_ref[i].astype(jnp.float32), (128, 128)).T
        hit = wanted[:, 0:1] == ids
        target = jnp.sum(jnp.where(hit, block, 0.0), axis=1, keepdims=True)
        lane = lax.broadcasted_iota(jnp.int32, (128, 128), 1)
        three = jnp.where(lane == 0, top, jnp.where(lane == 1, total, target))
        stats[i] = three.T[0:8]

    join_e[e] = stats[e]
    small += arrived(swap_small(
        join_e, lambda k: (stats.at[(e + k) % 8], join_e.at[e]), expert_peer, je_send, je_recv
    ))
    top, total, target = merge_stats(join_e)
    join_t[t, 0:1] = top
    join_t[t, 1:2] = total
    join_t[t, 2:3] = target
    join_t[t, 3:8] = jnp.zeros((5, 128), jnp.float32)
    small += arrived(swap_small(
        join_t, lambda k: (join_t.at[t], join_t.at[t]), tensor_peer, jt_send, jt_recv
    ))
    top, total, target = merge_stats(join_t)
    out_ref[...] = jnp.broadcast_to(top + jnp.log(total) - target, out_ref.shape)
    for c in small:
        c.wait_send()


CHUNKS = 4
SLOTS = 16
CHUNK_ROWS = 8 * SLOTS
Z_FIRST = (0, 80)
Y_FIRST = (80, 48)
HIDDEN_TILES = ((0, 256), (256, 256), (512, 256), (768, 128))


class Lane:
    def __init__(self, send, recv, chunk):
        self.send, self.recv, self.chunk, self.used, self.copies = send, recv, chunk, 0, []

    def start(self, src, dst, dev):
        c = remote(
            src, dst, self.send.at[self.chunk, self.used], self.recv.at[self.chunk, self.used], dev
        )
        self.used += 1
        c.start()
        self.copies.append(c)
        return c

    def finish(self):
        for c in self.copies:
            c.wait_send()


def expert_body(
    tok_ref, gain_ref, routes_ref, weights_ref, final_ref, tgt_ref,
    wg_hbm, wu_hbm, wd_hbm, head_hbm, out_ref,
    wg, wu, wd, head_t, sent, X, hidden, part, twin, ra1, ra2, ra3, rb1, rb2, rb3, back, sq,
    buf, acc, sq2, stats, join_e, join_t,
    w_sem, sq_send, sq_recv, g_send, g_recv, r_send, r_recv,
    h_send, h_recv, s2_send, s2_recv, je_send, je_recv, jt_send, jt_recv,
    scales, sc_send, sc_recv, slot_out, slot_in, so_send, so_recv, tw_send, tw_recv,
):
    me = place()
    s = lax.axis_index("seq")
    e = lax.axis_index("expert")
    t = lax.axis_index("tensor")
    y, zl = me["y"], t % 2
    f32, bf16 = jnp.float32, jnp.bfloat16
    loads = [
        pltpu.make_async_copy(src.at[0], dst, w_sem.at[i])
        for i, (src, dst) in enumerate(((wg_hbm, wg), (wu_hbm, wu), (wd_hbm, wd)))
    ]
    head_load = pltpu.make_async_copy(head_hbm, head_t, w_sem.at[3])
    for c in loads:
        c.start()
    head_load.start()
    twin_dev = (1 - s, e, t)
    pair_dev = (s, e, y * 2 + 1 - zl)

    def y_dev(by):
        return (s, e, ((y + by + 4) % 4) * 2 + zl)

    def at_y(by):
        return (y + by + 4) % 4

    greet(
        [tensor_peer(k) for k in range(1, 8)]
        + [expert_peer(k) for k in range(1, 8)]
        + [twin_dev, device_at(moved(me, "z", 2 * zl - 1))]
    )
    x = tok_ref[...].astype(f32)
    sq[t] = squares_row(x)
    weighted = (x * gain_ref[...]).astype(bf16)
    names = [routes_ref[j : j + 1, :] for j in range(2)]
    ids = lax.broadcasted_iota(jnp.int32, (8, 128), 0)
    named = ((names[0] == ids) | (names[1] == ids)).astype(f32)
    lower = (
        lax.broadcasted_iota(jnp.int32, (128, 128), 0)
        < lax.broadcasted_iota(jnp.int32, (128, 128), 1)
    ).astype(f32)
    earlier = jnp.dot(named, lower, preferred_element_type=f32)
    slot_ids = lax.broadcasted_iota(jnp.int32, (SLOTS, 128), 0).astype(f32)

    def selection(j, chunk, i):
        own = earlier[i : i + 1] == slot_ids + float(SLOTS * chunk)
        if j is None:
            hit = named[i : i + 1] > 0.5
        else:
            hit = names[j] == i
        return jnp.where(own & hit, 1.0, 0.0)

    for chunk in range(CHUNKS):
        pick = jnp.concatenate([selection(None, chunk, i) for i in range(8)], axis=0)
        sent[chunk] = jnp.dot(
            pick.astype(bf16), weighted, preferred_element_type=f32
        ).astype(bf16)
    pl.semaphore_wait(pltpu.get_barrier_semaphore(), 16)
    small = swap_small(sq, lambda k: (sq.at[t], sq.at[t]), tensor_peer, sq_send, sq_recv)

    def cols(first, n):
        return pl.ds(pl.multiple_of(first, 256), n)

    def rows_of(i):
        return pl.ds(pl.multiple_of(i * SLOTS, SLOTS), SLOTS)

    lanes = [Lane(g_send, g_recv, c) for c in range(CHUNKS)]
    sums = [Lane(r_send, r_recv, c) for c in range(CHUNKS)]
    own_cols = cols(t * 512, 512)
    arrivals = []
    for chunk in range(CHUNKS):
        X[chunk, s, rows_of(e), own_cols] = sent[chunk, rows_of(e), :]
        arrivals.append([
            lanes[chunk].start(
                sent.at[chunk, rows_of((e + k) % 8)],
                X.at[chunk, s, rows_of(e), own_cols],
                expert_peer(k),
            )
            for k in range(1, 8)
        ])

    def gather(chunk):
        lane = lanes[chunk]

        def view(rows, first, n):
            return X.at[chunk, s, pl.ds(*rows), cols(first, n)]

        def put(rows, first, n, dev):
            v = view(rows, first, n)
            return lane.start(v, v, dev)

        for c in arrivals[chunk]:
            c.wait_recv()
        az = put(Z_FIRST, t * 512, 512, pair_dev)
        by = [put(Y_FIRST, t * 512, 512, y_dev(d)) for d in (1, -1)]
        bz = [put(Y_FIRST, t * 512, 512, pair_dev)]
        yield
        az.wait_recv()
        ay = [put(Z_FIRST, y * 1024, 1024, y_dev(d)) for d in (1, -1)]
        twins = [put(Z_FIRST, y * 1024, 1024, twin_dev)]
        bh = []
        for side, d in ((0, 1), (1, -1)):
            by[side].wait_recv()
            first = (at_y(-d) * 2 + zl) * 512
            bh.append(put(Y_FIRST, first + 256 * side, 256, y_dev(d)))
            bz.append(put(Y_FIRST, first, 512, pair_dev))
        yield
        ah = []
        for side, d in ((0, 1), (1, -1)):
            ay[side].wait_recv()
            first = at_y(-d) * 1024
            ah.append(put(Z_FIRST, first + 512 * side, 512, y_dev(d)))
            twins.append(put(Z_FIRST, first, 1024, twin_dev))
        for c in bh:
            c.wait_recv()
        bz.append(put(Y_FIRST, (at_y(2) * 2 + zl) * 512, 512, pair_dev))
        for i, d in enumerate((0, -1, 1)):
            bz[i].wait_recv()
            twins.append(put(Y_FIRST, at_y(d) * 1024, 1024, twin_dev))
        yield
        for c in ah:
            c.wait_recv()
        twins.append(put(Z_FIRST, at_y(2) * 1024, 1024, twin_dev))
        bz[3].wait_recv()
        twins.append(put(Y_FIRST, at_y(2) * 1024, 1024, twin_dev))
        yield
        for c in twins:
            c.wait_recv()

    pending = [[] for _ in range(CHUNKS)]

    def compute(chunk):
        def up_step(first, n):
            def step():
                rows = X[chunk].reshape(2 * CHUNK_ROWS, 4096)
                scale = slot_in[:, :, chunk].reshape(2 * CHUNK_ROWS, 128)[:, 0:1]
                gate = jnp.dot(rows, wg[:, first : first + n], preferred_element_type=f32) * scale
                up = jnp.dot(rows, wu[:, first : first + n], preferred_element_type=f32) * scale
                hidden[:, first : first + n] = (gate / (1.0 + jnp.exp(-gate)) * up).astype(bf16)
            return step

        def down_step(k):
            def step():
                first = k * 512
                done = jnp.dot(hidden[...], wd[:, first : first + 512], preferred_element_type=f32)
                part[chunk, :, :, first : first + 512] = done.astype(bf16).reshape(
                    2, CHUNK_ROWS, 512
                )
                pending[chunk].append(
                    sums[chunk].start(
                        part.at[chunk, 1 - s, :, pl.ds(first, 512)],
                        twin.at[chunk, :, pl.ds(first, 512)],
                        twin_dev,
                    )
                )
            return step

        return [up_step(*tile) for tile in HIDDEN_TILES] + [down_step(k) for k in range(8)]

    def reduce(chunk):
        lane = sums[chunk]

        def add(rows, first, n, *others):
            block = part[chunk, s, pl.ds(*rows), cols(first, n)].astype(f32)
            for o in others:
                block = block + o.astype(f32)
            part[chunk, s, pl.ds(*rows), cols(first, n)] = block.astype(bf16)

        def put(rows, first, n, dst, dev):
            return lane.start(part.at[chunk, s, pl.ds(*rows), cols(first, n)], dst, dev)

        for k in range(8):
            pending[chunk][k].wait_recv()
            first = k * 512
            part[chunk, s, :, first : first + 512] = (
                part[chunk, s, :, first : first + 512].astype(f32)
                + twin[chunk, :, first : first + 512].astype(f32)
            ).astype(bf16)
        a1 = [
            put(Z_FIRST, at_y(2) * 1024 + 512 * h, 512, ra1.at[chunk, h], y_dev(d))
            for h, d in ((0, -1), (1, 1))
        ]
        b1 = [
            put(Y_FIRST, (at_y(d) * 2 + 1 - zl) * 512, 512, rb1.at[chunk, i], pair_dev)
            for i, d in enumerate((2, 1, -1, 0))
        ]
        yield
        b1[0].wait_recv()
        add(Y_FIRST, (at_y(2) * 2 + zl) * 512, 512, rb1[chunk, 0])
        b2 = [
            put(Y_FIRST, (at_y(2) * 2 + zl) * 512 + 256 * h, 256, rb2.at[chunk, h], y_dev(d))
            for h, d in ((0, -1), (1, 1))
        ]
        a2 = []
        for h, d in ((0, -1), (1, 1)):
            a1[h].wait_recv()
            add(Z_FIRST, at_y(d) * 1024 + 512 * h, 512, ra1[chunk, h])
            a2.append(put(Z_FIRST, at_y(d) * 1024, 1024, ra2.at[chunk, h], y_dev(d)))
        yield
        for i, d in ((1, 1), (2, -1), (3, 0)):
            b1[i].wait_recv()
            add(Y_FIRST, (at_y(d) * 2 + zl) * 512, 512, rb1[chunk, i])
        b3 = []
        for h, d in ((0, -1), (1, 1)):
            b2[h].wait_recv()
            first = (at_y(d) * 2 + zl) * 512
            add(Y_FIRST, first + 256 * h, 256, rb2[chunk, h])
            b3.append(put(Y_FIRST, first, 512, rb3.at[chunk, h], y_dev(d)))
        yield
        for c in a2:
            c.wait_recv()
        add(Z_FIRST, y * 1024, 1024, ra2[chunk, 0], ra2[chunk, 1])
        a3 = put(Z_FIRST, (y * 2 + 1 - zl) * 512, 512, ra3.at[chunk], pair_dev)
        for c in b3:
            c.wait_recv()
        add(Y_FIRST, t * 512, 512, rb3[chunk, 0], rb3[chunk, 1])
        yield
        a3.wait_recv()
        add(Z_FIRST, t * 512, 512, ra3[chunk])
        back[chunk, rows_of(e), :] = part[chunk, s, rows_of(e), own_cols]
        homes = [
            lane.start(
                part.at[chunk, s, rows_of((e + k) % 8), own_cols],
                back.at[chunk, rows_of(e)],
                expert_peer(k),
            )
            for k in range(1, 8)
        ]
        yield
        for c in homes:
            c.wait_recv()

    g = [gather(c) for c in range(CHUNKS)]
    r = [reduce(c) for c in range(CHUNKS)]

    def weave(steps, moves):
        done = 0
        for i, step in enumerate(steps):
            step()
            upto = (i + 1) * len(moves) // len(steps)
            for m in moves[done:upto]:
                next(m, None)
            done = upto

    def advance(order, moves):
        for c in order:
            next(moves[c], None)

    advance((0, 1), g)
    arrived(small)
    factor = lax.rsqrt(sum(sq[i] for i in range(8))[0:1] / 4096.0 + epsilon)
    for i in range(8):
        for chunk in range(CHUNKS):
            picked = jnp.sum(selection(None, chunk, i) * factor, axis=1, keepdims=True)
            slot_out[i, chunk] = jnp.broadcast_to(picked, (SLOTS, 128))
    slot_in[s, e] = slot_out[e]
    factors = swap_small(
        slot_in, lambda k: (slot_out.at[(e + k) % 8], slot_in.at[s, e]), expert_peer,
        so_send, so_recv,
    )
    advance((0, 2, 1, 0, 3, 2), g)
    arrived(factors)
    crossing = remote(slot_in.at[s], slot_in.at[s], tw_send.at[0], tw_recv.at[0], twin_dev)
    crossing.start()
    advance((1, 0, 3, 2, 0), g)
    crossing.wait_recv()
    small += factors + [crossing]
    for c in loads:
        c.wait()
    weave(compute(0), [g[1], g[3], g[2], g[1]])
    weave(compute(1), [r[0], g[3], g[2], r[0], g[3]])
    weave(compute(2), [r[0], r[1], r[0], r[1]])
    weave(compute(3), [r[0], r[1], r[2], r[0], r[1], r[2]])
    advance((3, 1, 2, 3, 1, 2, 3, 2, 3, 2, 3, 3), r)

    mixed = jnp.zeros((128, 512), f32)
    for j in range(2):
        total = jnp.zeros((128, 512), f32)
        for chunk in range(CHUNKS):
            pick = jnp.concatenate([selection(j, chunk, i) for i in range(8)], axis=0)
            total = total + lax.dot_general(
                pick.T.astype(bf16), back[chunk], (((1,), (0,)), ((), ())),
                preferred_element_type=f32,
            )
        mixed = mixed + weights_ref[:, j : j + 1] * total
    residual = (x + mixed).astype(bf16).astype(f32)
    head_part(
        residual, final_ref, head_load, head_t, tgt_ref, out_ref, buf, acc, sq2, stats, join_e, join_t,
        h_send, h_recv, s2_send, s2_recv, je_send, je_recv, jt_send, jt_recv,
        scales, sc_send, sc_recv,
    )
    for c in small:
        c.wait_send()
    for lane in lanes + sums:
        lane.finish()


def layer_loss(
    tokens, gain, routes, route_weights, final_gain, targets, w_gate, w_up, w_down, head_weight
):
    vmem = pl.BlockSpec(memory_space=pltpu.VMEM)
    hbm = pl.BlockSpec(memory_space=pl.ANY)
    sem = pltpu.SemaphoreType.DMA
    bf16, f32 = jnp.bfloat16, jnp.float32
    a, b = Z_FIRST[1], Y_FIRST[1]
    return pl.pallas_call(
        expert_body,
        out_shape=jax.ShapeDtypeStruct((8, 128), f32),
        in_specs=[vmem] * 6 + [hbm] * 4,
        out_specs=vmem,
        scratch_shapes=[
            pltpu.VMEM((4096, 896), bf16),
            pltpu.VMEM((4096, 896), bf16),
            pltpu.VMEM((896, 4096), bf16),
            pltpu.VMEM((500, 4096), bf16),
            pltpu.VMEM((CHUNKS, CHUNK_ROWS, 512), bf16),
            pltpu.VMEM((CHUNKS, 2, CHUNK_ROWS, 4096), bf16),
            pltpu.VMEM((2 * CHUNK_ROWS, 896), bf16),
            pltpu.VMEM((CHUNKS, 2, CHUNK_ROWS, 4096), bf16),
            pltpu.VMEM((CHUNKS, CHUNK_ROWS, 4096), bf16),
            pltpu.VMEM((CHUNKS, 2, a, 512), bf16),
            pltpu.VMEM((CHUNKS, 2, a, 1024), bf16),
            pltpu.VMEM((CHUNKS, a, 512), bf16),
            pltpu.VMEM((CHUNKS, 4, b, 512), bf16),
            pltpu.VMEM((CHUNKS, 2, b, 256), bf16),
            pltpu.VMEM((CHUNKS, 2, b, 512), bf16),
            pltpu.VMEM((CHUNKS, CHUNK_ROWS, 512), bf16),
            pltpu.VMEM((8, 8, 128), f32),
            pltpu.VMEM((2, 4, 4, 2, 128, 512), bf16),
            pltpu.VMEM((1024, 500), f32),
            pltpu.VMEM((8, 8, 128), f32),
            pltpu.VMEM((8, 8, 128), f32),
            pltpu.VMEM((8, 8, 128), f32),
            pltpu.VMEM((8, 8, 128), f32),
            sem((4,)), sem((7,)), sem((7,)),
            sem((CHUNKS, 32)), sem((CHUNKS, 32)), sem((CHUNKS, 32)), sem((CHUNKS, 32)),
            sem((3, 3, 4)), sem((3, 3, 4)),
            sem((7,)), sem((7,)), sem((7,)), sem((7,)), sem((7,)), sem((7,)),
            pltpu.VMEM((8, 8, 128), f32), sem((7,)), sem((7,)),
            pltpu.VMEM((8, CHUNKS, SLOTS, 128), f32),
            pltpu.VMEM((2, 8, CHUNKS, SLOTS, 128), f32),
            sem((7,)), sem((7,)), sem((1,)), sem((1,)),
        ],
        compiler_params=pltpu.CompilerParams(
            collective_id=0, has_side_effects=True, vmem_limit_bytes=67043328
        ),
        name="layer_loss",
    )(
        tokens, gain.reshape(1, 512), routes.T, route_weights, final_gain.reshape(1, 512),
        targets.reshape(8, 1, 128), w_gate, w_up, w_down, head_weight.T,
    )


def on_device(
    tokens, routes, route_weights, norm_gain, final_gain, w_gate, w_up, w_down, head_weight, targets
):
    loss = layer_loss(
        tokens, norm_gain, routes, route_weights, final_gain, targets, w_gate, w_up, w_down,
        head_weight,
    )[0]
    own_rows = tokens.shape[0] // 8
    return lax.dynamic_slice_in_dim(loss, lax.axis_index("tensor") * own_rows, own_rows)


def solution(mesh):
    return jax.shard_map(
        on_device,
        mesh=mesh,
        in_specs=(
            P(("seq", "expert"), "tensor"),
            P(("seq", "expert"), None),
            P(("seq", "expert"), None),
            P("tensor"),
            P("tensor"),
            P("expert", None, ("seq", "tensor")),
            P("expert", None, ("seq", "tensor")),
            P("expert", ("seq", "tensor"), None),
            P(None, ("expert", "tensor")),
            P("seq"),
        ),
        out_specs=P(("seq", "expert", "tensor")),
        check_vma=False,
    )
```

```python
import functools
import jax
import jax.numpy as jnp
from jax import lax
from jax.experimental import pallas as pl
from jax.experimental.pallas import tpu as pltpu
from jax.sharding import PartitionSpec as P

epsilon = 1e-05
MESH = pl.DeviceIdType.MESH
PIECES = (
    ((0, 32, 0, 512), (32, 16, 0, 384)),
    ((48, 32, 0, 512), (80, 16, 0, 384)),
    ((96, 32, 0, 512), (32, 16, 384, 128), (80, 16, 384, 128)),
)
PASSED = (
    (((0, 32, 0, 256), 0), ((32, 16, 0, 128), 1)), (((0, 32, 256, 256), 0), ((32, 16, 128, 256), 1)),
    (((48, 32, 0, 256), 0), ((80, 16, 0, 256), 1)), (((48, 32, 256, 256), 0), ((80, 16, 256, 128), 1)),
    (((96, 32, 0, 256), 0), ((32, 16, 384, 128), 1)), (((96, 32, 256, 256), 0), ((80, 16, 384, 128), 2)),
)
AXES = "xyz"


def place():
    e = lax.axis_index("expert")
    t = lax.axis_index("tensor")
    return {"x": e % 4, "y": t // 2, "z": (e // 4) * 2 + t % 2}


def device_at(pos):
    z = pos["z"]
    return (lax.axis_index("seq"), (z // 2) * 4 + pos["x"], pos["y"] * 2 + z % 2)


def moved(pos, axis, by):
    out = dict(pos)
    out[axis] = (pos[axis] + by + 4) % 4
    return out


def tensor_peer(k):
    return (lax.axis_index("seq"), lax.axis_index("expert"), (lax.axis_index("tensor") + k) % 8)


def expert_peer(k):
    return (lax.axis_index("seq"), (lax.axis_index("expert") + k) % 8, lax.axis_index("tensor"))


def remote(src, dst, send, recv, dev):
    return pltpu.make_async_remote_copy(
        src_ref=src, dst_ref=dst, send_sem=send, recv_sem=recv, device_id=dev, device_id_type=MESH
    )


def greet(peers):
    barrier = pltpu.get_barrier_semaphore()
    for dev in peers:
        pl.semaphore_signal(barrier, inc=1, device_id=dev, device_id_type=MESH)


def region(buf, full, pos, piece):
    row, rows, col, cols = piece
    z = pos["z"]
    zh = pl.ds(0, 2) if "z" in full else z // 2
    zl = pl.ds(0, 2) if "z" in full else z % 2
    x = pl.ds(0, 4) if "x" in full else pos["x"]
    y = pl.ds(0, 4) if "y" in full else pos["y"]
    return buf.at[zh, x, y, zl, pl.ds(row, rows), pl.ds(col, cols)]


def ring_gather(buf, send, recv):
    me = place()
    copies = []
    for phase in range(3):
        first = {}
        used = [0, 0, 0]

        def put(color, pos, full, piece, axis, by):
            ref = region(buf, full, pos, piece)
            k = used[color]
            used[color] += 1
            c = remote(
                ref, ref, send.at[color, phase, k], recv.at[color, phase, k],
                device_at(moved(me, axis, by)),
            )
            c.start()
            copies.append(c)
            return c

        lines = [
            (color, AXES[(color + phase) % 3], [AXES[(color + p) % 3] for p in range(phase)])
            for color in range(3)
        ]
        for color, axis, full in lines:
            for i, piece in enumerate(PIECES[color]):
                for side, by in ((0, 1), (1, -1)):
                    first[color, side, i] = put(color, me, full, piece, axis, by)
        second = []
        waited = set()
        for turn in range(2):
            for color, axis, full in lines:
                for side, by in ((0, 1), (1, -1)):
                    piece, source = PASSED[2 * color + side][turn]
                    if (color, side, source) not in waited:
                        waited.add((color, side, source))
                        first[color, side, source].wait_recv()
                    second.append(put(color, moved(me, axis, -by), full, piece, axis, by))
        for key in first:
            if key not in waited:
                first[key].wait_recv()
        for c in second:
            c.wait_recv()
        yield
    for c in copies:
        c.wait_send()


def swap_small(buf, mine, peer, send, recv):
    copies = []
    for k in range(1, 8):
        src, dst = mine(k)
        c = remote(src, dst, send.at[k - 1], recv.at[k - 1], peer(k))
        c.start()
        copies.append(c)
    return copies


def arrived(copies):
    for c in copies:
        c.wait_recv()
    return copies


def squares_row(x):
    return jnp.broadcast_to(jnp.sum(x * x, axis=1, keepdims=True), (128, 128)).T[0:8]


def merge_stats(buf):
    tops = [buf[i, 0:1, :] for i in range(8)]
    top = functools.reduce(jnp.maximum, tops)
    total = sum(buf[i, 1:2, :] * jnp.exp(buf[i, 0:1, :] - top) for i in range(8))
    target = sum(buf[i, 2:3, :] for i in range(8))
    return top, total, target


def head_part(
    x, gain_ref, head_load, head_t, tgt_ref, out_ref, buf, sq, stats, join_e, join_t,
    send, recv, sq_send, sq_recv, je_send, je_recv, jt_send, jt_recv, scales, sc_send, sc_recv,
):
    me = place()
    e = lax.axis_index("expert")
    t = lax.axis_index("tensor")
    sq[t] = squares_row(x)
    buf[me["z"] // 2, me["x"], me["y"], me["z"] % 2] = (x * gain_ref[...]).astype(jnp.bfloat16)
    moves = ring_gather(buf, send, recv)
    small = swap_small(sq, lambda k: (sq.at[t], sq.at[t]), tensor_peer, sq_send, sq_recv)
    next(moves)
    arrived(small)
    scales[e] = lax.rsqrt(sum(sq[i] for i in range(8)) / 4096.0 + epsilon)
    spread = swap_small(
        scales, lambda k: (scales.at[e], scales.at[e]), expert_peer, sc_send, sc_recv
    )
    next(moves)
    next(moves)
    next(moves, None)
    small += arrived(spread)

    head_load.wait()
    start = (e * 8 + t) * 500

    def block_terms(i, block):
        column = jnp.broadcast_to(scales[i, 0:1, :], (128, 128)).T
        block = block * column[:, 0:1]
        top = jnp.max(block, axis=1, keepdims=True)
        total = jnp.sum(jnp.exp(block - top), axis=1, keepdims=True)
        ids = (lax.broadcasted_iota(jnp.int32, block.shape, 1) + start).astype(jnp.float32)
        wanted = jnp.broadcast_to(tgt_ref[i].astype(jnp.float32), (128, 128)).T
        target = jnp.sum(jnp.where(wanted[:, 0:1] == ids, block, 0.0), axis=1, keepdims=True)
        lane = lax.broadcasted_iota(jnp.int32, (128, 128), 1)
        three = jnp.where(lane == 0, top, jnp.where(lane == 1, total, target))
        stats[i] = three.T[0:8]

    @pl.loop(0, 2)
    def _(zh):
        for pair in range(2):
            logits = jnp.zeros((256, 500), jnp.float32)
            for k in range(8):
                piece = buf[zh, 2 * pair : 2 * pair + 2, k // 2, k % 2].reshape(256, 512)
                logits = logits + lax.dot_general(
                    piece, head_t[:, k * 512 : k * 512 + 512], (((1,), (1,)), ((), ())),
                    preferred_element_type=jnp.float32,
                )
            for j in range(2):
                block_terms(zh * 4 + 2 * pair + j, logits[128 * j : 128 * j + 128])

    join_e[e] = stats[e]
    small += arrived(swap_small(
        join_e, lambda k: (stats.at[(e + k) % 8], join_e.at[e]), expert_peer, je_send, je_recv
    ))
    top, total, target = merge_stats(join_e)
    join_t[t, 0:1] = top
    join_t[t, 1:2] = total
    join_t[t, 2:3] = target
    join_t[t, 3:8] = jnp.zeros((5, 128), jnp.float32)
    small += arrived(swap_small(
        join_t, lambda k: (join_t.at[t], join_t.at[t]), tensor_peer, jt_send, jt_recv
    ))
    top, total, target = merge_stats(join_t)
    out_ref[...] = jnp.broadcast_to(top + jnp.log(total) - target, out_ref.shape)
    for c in small:
        c.wait_send()


CHUNKS = 4
SLOTS = 16
CHUNK_ROWS = 8 * SLOTS
SPLITS = (80, 64, 80, 64)
HIDDEN_TILES = ((0, 256), (256, 256), (512, 256), (768, 128))


class Lane:
    def __init__(self, send, recv, chunk):
        self.send, self.recv, self.chunk, self.used, self.copies = send, recv, chunk, 0, []

    def start(self, src, dst, dev):
        c = remote(
            src, dst, self.send.at[self.chunk, self.used], self.recv.at[self.chunk, self.used], dev
        )
        self.used += 1
        c.start()
        self.copies.append(c)
        return c

    def finish(self):
        for c in self.copies:
            c.wait_send()


def parts_of(chunk):
    n = SPLITS[chunk]
    return (0, n), (n, CHUNK_ROWS - n)


def expert_body(
    tok_ref, gain_ref, routes_ref, weights_ref, final_ref, tgt_ref,
    wg_hbm, wu_hbm, wd_hbm, head_hbm, out_ref,
    wg, wu, wd, head_t, sent, X, hidden, part, twin, ra1, ra2, ra3, rb1, rb2, rb3, back, sq,
    buf, sq2, stats, join_e, join_t,
    w_sem, sq_send, sq_recv, g_send, g_recv, r_send, r_recv,
    h_send, h_recv, s2_send, s2_recv, je_send, je_recv, jt_send, jt_recv,
    scales, sc_send, sc_recv, slot_out, slot_in, so_send, so_recv, tw_send, tw_recv,
):
    me = place()
    s = lax.axis_index("seq")
    e = lax.axis_index("expert")
    t = lax.axis_index("tensor")
    y, zl = me["y"], t % 2
    f32, bf16 = jnp.float32, jnp.bfloat16
    loads = [
        pltpu.make_async_copy(src.at[0], dst, w_sem.at[i])
        for i, (src, dst) in enumerate(((wg_hbm, wg), (wu_hbm, wu), (wd_hbm, wd)))
    ]
    head_load = pltpu.make_async_copy(head_hbm, head_t, w_sem.at[3])
    for c in loads:
        c.start()
    head_load.start()
    twin_dev = (1 - s, e, t)
    pair_dev = (s, e, y * 2 + 1 - zl)

    def y_dev(by):
        return (s, e, ((y + by + 4) % 4) * 2 + zl)

    def at_y(by):
        return (y + by + 4) % 4

    greet(
        [tensor_peer(k) for k in range(1, 8)]
        + [expert_peer(k) for k in range(1, 8)]
        + [twin_dev, device_at(moved(me, "z", 2 * zl - 1))]
    )
    x = tok_ref[...].astype(f32)
    sq[t] = squares_row(x)
    weighted = (x * gain_ref[...]).astype(bf16)
    names = [routes_ref[j : j + 1, :] for j in range(2)]
    ids = lax.broadcasted_iota(jnp.int32, (8, 128), 0)
    named = ((names[0] == ids) | (names[1] == ids)).astype(f32)
    lower = (
        lax.broadcasted_iota(jnp.int32, (128, 128), 0)
        < lax.broadcasted_iota(jnp.int32, (128, 128), 1)
    ).astype(f32)
    earlier = jnp.dot(named, lower, preferred_element_type=f32)
    slot_ids = lax.broadcasted_iota(jnp.int32, (SLOTS, 128), 0).astype(f32)

    def selection(j, chunk, i):
        own = earlier[i : i + 1] == slot_ids + float(SLOTS * chunk)
        if j is None:
            hit = named[i : i + 1] > 0.5
        else:
            hit = names[j] == i
        return jnp.where(own & hit, 1.0, 0.0)

    for chunk in range(CHUNKS):
        pick = jnp.concatenate([selection(None, chunk, i) for i in range(8)], axis=0)
        sent[chunk] = jnp.dot(
            pick.astype(bf16), weighted, preferred_element_type=f32
        ).astype(bf16)
    pl.semaphore_wait(pltpu.get_barrier_semaphore(), 16)
    small = swap_small(sq, lambda k: (sq.at[t], sq.at[t]), tensor_peer, sq_send, sq_recv)

    def cols(first, n):
        return pl.ds(pl.multiple_of(first, 256), n)

    def rows_of(i):
        return pl.ds(pl.multiple_of(i * SLOTS, SLOTS), SLOTS)

    lanes = [Lane(g_send, g_recv, c) for c in range(CHUNKS)]
    sums = [Lane(r_send, r_recv, c) for c in range(CHUNKS)]
    own_cols = cols(t * 512, 512)
    arrivals = []
    for chunk in range(CHUNKS):
        X[chunk, s, rows_of(e), own_cols] = sent[chunk, rows_of(e), :]
        arrivals.append([
            lanes[chunk].start(
                sent.at[chunk, rows_of((e + k) % 8)],
                X.at[chunk, s, rows_of(e), own_cols],
                expert_peer(k),
            )
            for k in range(1, 8)
        ])

    def gather(chunk):
        lane = lanes[chunk]
        z_rows, y_rows = parts_of(chunk)

        def view(rows, first, n):
            return X.at[chunk, s, pl.ds(*rows), cols(first, n)]

        def put(rows, first, n, dev):
            v = view(rows, first, n)
            return lane.start(v, v, dev)

        for c in arrivals[chunk]:
            c.wait_recv()
        az = put(z_rows, t * 512, 512, pair_dev)
        by = [put(y_rows, t * 512, 512, y_dev(d)) for d in (1, -1)]
        bz = [put(y_rows, t * 512, 512, pair_dev)]
        yield
        az.wait_recv()
        ay = [put(z_rows, y * 1024, 1024, y_dev(d)) for d in (1, -1)]
        twins = [put(z_rows, y * 1024, 1024, twin_dev)]
        bh = []
        for side, d in ((0, 1), (1, -1)):
            by[side].wait_recv()
            first = (at_y(-d) * 2 + zl) * 512
            bh.append(put(y_rows, first + 256 * side, 256, y_dev(d)))
            bz.append(put(y_rows, first, 512, pair_dev))
        yield
        ah = []
        for side, d in ((0, 1), (1, -1)):
            ay[side].wait_recv()
            first = at_y(-d) * 1024
            ah.append(put(z_rows, first + 512 * side, 512, y_dev(d)))
            twins.append(put(z_rows, first, 1024, twin_dev))
        for c in bh:
            c.wait_recv()
        bz.append(put(y_rows, (at_y(2) * 2 + zl) * 512, 512, pair_dev))
        for i, d in enumerate((0, -1, 1)):
            bz[i].wait_recv()
            twins.append(put(y_rows, at_y(d) * 1024, 1024, twin_dev))
        yield
        for c in ah:
            c.wait_recv()
        twins.append(put(z_rows, at_y(2) * 1024, 1024, twin_dev))
        bz[3].wait_recv()
        twins.append(put(y_rows, at_y(2) * 1024, 1024, twin_dev))
        yield
        for c in twins:
            c.wait_recv()

    pending = [[] for _ in range(CHUNKS)]

    def compute(chunk):
        def up_step(first, n):
            def step():
                rows = X[chunk].reshape(2 * CHUNK_ROWS, 4096)
                scale = slot_in[:, :, chunk].reshape(2 * CHUNK_ROWS, 128)[:, 0:1]
                gate = jnp.dot(rows, wg[:, first : first + n], preferred_element_type=f32) * scale
                up = jnp.dot(rows, wu[:, first : first + n], preferred_element_type=f32) * scale
                hidden[:, first : first + n] = (gate / (1.0 + jnp.exp(-gate)) * up).astype(bf16)
            return step

        def down_step(k):
            def step():
                first = k * 512
                done = jnp.dot(hidden[...], wd[:, first : first + 512], preferred_element_type=f32)
                part[chunk, :, :, first : first + 512] = done.astype(bf16).reshape(
                    2, CHUNK_ROWS, 512
                )
                pending[chunk].append(
                    sums[chunk].start(
                        part.at[chunk, 1 - s, :, pl.ds(first, 512)],
                        twin.at[chunk, :, pl.ds(first, 512)],
                        twin_dev,
                    )
                )
            return step

        return [up_step(*tile) for tile in HIDDEN_TILES] + [down_step(k) for k in range(8)]

    def reduce(chunk):
        lane = sums[chunk]
        z_rows, y_rows = parts_of(chunk)

        def add(rows, first, n, *others):
            block = part[chunk, s, pl.ds(*rows), cols(first, n)].astype(f32)
            for o in others:
                block = block + o.astype(f32)
            part[chunk, s, pl.ds(*rows), cols(first, n)] = block.astype(bf16)

        def put(rows, first, n, dst, dev):
            return lane.start(part.at[chunk, s, pl.ds(*rows), cols(first, n)], dst, dev)

        for k in range(8):
            pending[chunk][k].wait_recv()
            first = k * 512
            part[chunk, s, :, first : first + 512] = (
                part[chunk, s, :, first : first + 512].astype(f32)
                + twin[chunk, :, first : first + 512].astype(f32)
            ).astype(bf16)
        a1 = [
            put(z_rows, at_y(2) * 1024 + 512 * h, 512, ra1.at[chunk, h, pl.ds(0, z_rows[1])], y_dev(d))
            for h, d in ((0, -1), (1, 1))
        ]
        b1 = [
            put(y_rows, (at_y(d) * 2 + 1 - zl) * 512, 512, rb1.at[chunk, i, pl.ds(0, y_rows[1])], pair_dev)
            for i, d in enumerate((2, 1, -1, 0))
        ]
        yield
        b1[0].wait_recv()
        add(y_rows, (at_y(2) * 2 + zl) * 512, 512, rb1[chunk, 0, : y_rows[1]])
        b2 = [
            put(y_rows, (at_y(2) * 2 + zl) * 512 + 256 * h, 256, rb2.at[chunk, h, pl.ds(0, y_rows[1])], y_dev(d))
            for h, d in ((0, -1), (1, 1))
        ]
        a2 = []
        for h, d in ((0, -1), (1, 1)):
            a1[h].wait_recv()
            add(z_rows, at_y(d) * 1024 + 512 * h, 512, ra1[chunk, h, : z_rows[1]])
            a2.append(put(z_rows, at_y(d) * 1024, 1024, ra2.at[chunk, h, pl.ds(0, z_rows[1])], y_dev(d)))
        yield
        for i, d in ((1, 1), (2, -1), (3, 0)):
            b1[i].wait_recv()
            add(y_rows, (at_y(d) * 2 + zl) * 512, 512, rb1[chunk, i, : y_rows[1]])
        b3 = []
        for h, d in ((0, -1), (1, 1)):
            b2[h].wait_recv()
            first = (at_y(d) * 2 + zl) * 512
            add(y_rows, first + 256 * h, 256, rb2[chunk, h, : y_rows[1]])
            b3.append(put(y_rows, first, 512, rb3.at[chunk, h, pl.ds(0, y_rows[1])], y_dev(d)))
        yield
        for c in a2:
            c.wait_recv()
        add(z_rows, y * 1024, 1024, ra2[chunk, 0, : z_rows[1]], ra2[chunk, 1, : z_rows[1]])
        a3 = put(z_rows, (y * 2 + 1 - zl) * 512, 512, ra3.at[chunk, pl.ds(0, z_rows[1])], pair_dev)
        for c in b3:
            c.wait_recv()
        add(y_rows, t * 512, 512, rb3[chunk, 0, : y_rows[1]], rb3[chunk, 1, : y_rows[1]])
        yield
        a3.wait_recv()
        add(z_rows, t * 512, 512, ra3[chunk, : z_rows[1]])
        back[chunk, rows_of(e), :] = part[chunk, s, rows_of(e), own_cols]
        homes = [
            lane.start(
                part.at[chunk, s, rows_of((e + k) % 8), own_cols],
                back.at[chunk, rows_of(e)],
                expert_peer(k),
            )
            for k in range(1, 8)
        ]
        yield
        for c in homes:
            c.wait_recv()

    g = [gather(c) for c in range(CHUNKS)]
    r = [reduce(c) for c in range(CHUNKS)]

    def weave(steps, moves):
        done = 0
        for i, step in enumerate(steps):
            step()
            upto = (i + 1) * len(moves) // len(steps)
            for m in moves[done:upto]:
                next(m, None)
            done = upto

    def advance(order, moves):
        for c in order:
            next(moves[c], None)

    advance((0, 1), g)
    arrived(small)
    factor = lax.rsqrt(sum(sq[i] for i in range(8))[0:1] / 4096.0 + epsilon)
    for i in range(8):
        for chunk in range(CHUNKS):
            picked = jnp.sum(selection(None, chunk, i) * factor, axis=1, keepdims=True)
            slot_out[i, chunk] = jnp.broadcast_to(picked, (SLOTS, 128))
    slot_in[s, e] = slot_out[e]
    factors = swap_small(
        slot_in, lambda k: (slot_out.at[(e + k) % 8], slot_in.at[s, e]), expert_peer,
        so_send, so_recv,
    )
    advance((0, 2, 1, 0, 3, 2), g)
    arrived(factors)
    crossing = remote(slot_in.at[s], slot_in.at[s], tw_send.at[0], tw_recv.at[0], twin_dev)
    crossing.start()
    advance((1, 0, 3, 2, 0), g)
    crossing.wait_recv()
    small += factors + [crossing]
    for c in loads:
        c.wait()
    weave(compute(0), [g[1], g[3], g[2], g[1]])
    weave(compute(1), [r[0], g[3], g[2], r[0], g[3]])
    weave(compute(2), [r[0], r[1], r[0], r[1]])
    weave(compute(3), [r[0], r[1], r[2], r[0], r[1], r[2]])
    advance((3, 1, 2, 3, 1, 2, 3, 2, 3, 2, 3, 3), r)

    mixed = jnp.zeros((128, 512), f32)
    for j in range(2):
        total = jnp.zeros((128, 512), f32)
        for chunk in range(CHUNKS):
            pick = jnp.concatenate([selection(j, chunk, i) for i in range(8)], axis=0)
            total = total + lax.dot_general(
                pick.T.astype(bf16), back[chunk], (((1,), (0,)), ((), ())),
                preferred_element_type=f32,
            )
        mixed = mixed + weights_ref[:, j : j + 1] * total
    residual = (x + mixed).astype(bf16).astype(f32)
    head_part(
        residual, final_ref, head_load, head_t, tgt_ref, out_ref, buf, sq2, stats, join_e, join_t,
        h_send, h_recv, s2_send, s2_recv, je_send, je_recv, jt_send, jt_recv,
        scales, sc_send, sc_recv,
    )
    for c in small:
        c.wait_send()
    for lane in lanes + sums:
        lane.finish()


def layer_loss(
    tokens, gain, routes, route_weights, final_gain, targets, w_gate, w_up, w_down, head_weight
):
    vmem = pl.BlockSpec(memory_space=pltpu.VMEM)
    hbm = pl.BlockSpec(memory_space=pl.ANY)
    sem = pltpu.SemaphoreType.DMA
    bf16, f32 = jnp.bfloat16, jnp.float32
    a, b = max(SPLITS), CHUNK_ROWS - min(SPLITS)
    return pl.pallas_call(
        expert_body,
        out_shape=jax.ShapeDtypeStruct((8, 128), f32),
        in_specs=[vmem] * 6 + [hbm] * 4,
        out_specs=vmem,
        scratch_shapes=[
            pltpu.VMEM((4096, 896), bf16),
            pltpu.VMEM((4096, 896), bf16),
            pltpu.VMEM((896, 4096), bf16),
            pltpu.VMEM((500, 4096), bf16),
            pltpu.VMEM((CHUNKS, CHUNK_ROWS, 512), bf16),
            pltpu.VMEM((CHUNKS, 2, CHUNK_ROWS, 4096), bf16),
            pltpu.VMEM((2 * CHUNK_ROWS, 896), bf16),
            pltpu.VMEM((CHUNKS, 2, CHUNK_ROWS, 4096), bf16),
            pltpu.VMEM((CHUNKS, CHUNK_ROWS, 4096), bf16),
            pltpu.VMEM((CHUNKS, 2, a, 512), bf16),
            pltpu.VMEM((CHUNKS, 2, a, 1024), bf16),
            pltpu.VMEM((CHUNKS, a, 512), bf16),
            pltpu.VMEM((CHUNKS, 4, b, 512), bf16),
            pltpu.VMEM((CHUNKS, 2, b, 256), bf16),
            pltpu.VMEM((CHUNKS, 2, b, 512), bf16),
            pltpu.VMEM((CHUNKS, CHUNK_ROWS, 512), bf16),
            pltpu.VMEM((8, 8, 128), f32),
            pltpu.VMEM((2, 4, 4, 2, 128, 512), bf16),
            pltpu.VMEM((8, 8, 128), f32),
            pltpu.VMEM((8, 8, 128), f32),
            pltpu.VMEM((8, 8, 128), f32),
            pltpu.VMEM((8, 8, 128), f32),
            sem((4,)), sem((7,)), sem((7,)),
            sem((CHUNKS, 32)), sem((CHUNKS, 32)), sem((CHUNKS, 32)), sem((CHUNKS, 32)),
            sem((3, 3, 10)), sem((3, 3, 10)),
            sem((7,)), sem((7,)), sem((7,)), sem((7,)), sem((7,)), sem((7,)),
            pltpu.VMEM((8, 8, 128), f32), sem((7,)), sem((7,)),
            pltpu.VMEM((8, CHUNKS, SLOTS, 128), f32),
            pltpu.VMEM((2, 8, CHUNKS, SLOTS, 128), f32),
            sem((7,)), sem((7,)), sem((1,)), sem((1,)),
        ],
        compiler_params=pltpu.CompilerParams(
            collective_id=0, has_side_effects=True, vmem_limit_bytes=67043328
        ),
        name="layer_loss",
    )(
        tokens, gain.reshape(1, 512), routes.T, route_weights, final_gain.reshape(1, 512),
        targets.reshape(8, 1, 128), w_gate, w_up, w_down, head_weight.T,
    )


def on_device(
    tokens, routes, route_weights, norm_gain, final_gain, w_gate, w_up, w_down, head_weight, targets
):
    loss = layer_loss(
        tokens, norm_gain, routes, route_weights, final_gain, targets, w_gate, w_up, w_down,
        head_weight,
    )[0]
    own_rows = tokens.shape[0] // 8
    return lax.dynamic_slice_in_dim(loss, lax.axis_index("tensor") * own_rows, own_rows)


def solution(mesh):
    return jax.shard_map(
        on_device,
        mesh=mesh,
        in_specs=(
            P(("seq", "expert"), "tensor"),
            P(("seq", "expert"), None),
            P(("seq", "expert"), None),
            P("tensor"),
            P("tensor"),
            P("expert", None, ("seq", "tensor")),
            P("expert", None, ("seq", "tensor")),
            P("expert", ("seq", "tensor"), None),
            P(None, ("expert", "tensor")),
            P("seq"),
        ),
        out_specs=P(("seq", "expert", "tensor")),
        check_vma=False,
    )
```
